32 devices in a mesh: grp: 2 (over x), ma: 16 (over z, y, core).
Axes of the slice: x: 2, y: 2, z: 4, core: 2. Of those that a mesh axis runs over, the one named last changes fastest.
Arguments:
- vis: float32 [16384, 2, 256], P(('grp', 'ma')), parts along dimension 0, may hold values from -6 to 6
- transfer: bfloat16 [32, 2, 256, 1024], P(('grp', 'ma')), parts along dimension 0, may hold values from -0.1875 to 0.1875
- band_start: int32 [2], P('grp'), parts along dimension 0, may hold values from 0 to 8176
- comp_index: int32 [2048], P(('grp', 'ma')), parts along dimension 0, may hold values from 0 to 16383
- comp_amp: int32 [2048, 2], P(('grp', 'ma')), parts along dimension 0, may hold values from -4096 to 4096
Outputs:
- residual_alm: float32 [32, 2, 1024], P(('grp', 'ma')), parts along dimension 0
The draws below stay inside these ranges and needn't reach their ends.
There are 2 independent parts, one for each index of `grp`. The reference program is written for one: setup_inputs(seed, part) draws one part's arguments, and reference() takes and returns one part's arrays. A program takes and returns all parts, laid end to end along the dimension named above; each array names one. Nothing has to cross between parts.
All inputs are finite; a program needn't handle non-finite values.
Results may differ from the reference program's by a relative error of at most 0.003.
Values sent between devices are 32-bit elements; how exact they have to be, the bound alone decides.
No kernel may reach another device: no remote copies, remote signals or barrier semaphores. Data moves between devices by JAX's collectives and lax.ppermute only.
A program may use at most 64 MiB of HBM per device.

```python
import math
import jax
import jax.numpy as jnp
from jax import lax

SIDEREAL_TICKS = 8192
L = 1024
BL = 256
MBAND = 16
NCOMP = 1024


def plant(result, stream_key, low, top_value):
    spot = [jax.random.randint(jax.random.fold_in(stream_key, axis), (), 0, length) for axis, length in enumerate(result.shape)]
    longest = result.shape.index(max(result.shape))
    beside = spot[:longest] + [(spot[longest] + 1) % result.shape[longest]] + spot[longest + 1:]
    return result.at[tuple(spot)].set(low).at[tuple(beside)].set(top_value)


def shard_levels(own_key, extent, shards, low, high):
    gain, own = 1.0, jax.random.fold_in(own_key, 6)
    for position, blocks in shards:
        draws = jnp.exp(jax.random.uniform(jax.random.fold_in(own, position), (blocks,), jnp.float32, low / len(shards), high / len(shards)))
        gain = gain * jnp.repeat(draws, extent[position] // blocks).reshape([-1 if axis == position else 1 for axis in range(len(extent))])
    return gain


def centred(stream_key, extent, scale, limit, pieces=(), kind=jnp.bfloat16):
    array = scale * jax.random.normal(stream_key, extent, jnp.float32)
    if pieces:
        array = array * shard_levels(stream_key, extent, pieces, -0.22, 0.18)
    return jnp.clip(array, -limit, limit).astype(kind)


def setup_inputs(seed: int = 0, part: int = 0) -> dict:
    key_list = jax.random.split(jax.random.key(seed), 6)
    part_keys = jax.random.split(jax.random.fold_in(key_list[5], part), 6)
    return {
        "vis": centred(part_keys[0], (SIDEREAL_TICKS, 2, BL), 1.0, 6.0, ((0, 16),), jnp.float32),
        "transfer": centred(part_keys[1], (MBAND, 2, BL, L), L ** -0.5, 0.1875, ((0, 16),)),
        "band_start": jax.random.randint(part_keys[2], (1,), 0, SIDEREAL_TICKS - MBAND + 1).astype(jnp.int32),
        "comp_index": plant(jax.random.randint(part_keys[3], (NCOMP,), 0, MBAND * L), jax.random.fold_in(part_keys[3], 1), 0, (MBAND * L) - 1).astype(jnp.int32),
        "comp_amp": plant(jax.random.randint(part_keys[4], (NCOMP, 2), -4096, 4097), jax.random.fold_in(part_keys[4], 1), -4096, 4096).astype(jnp.int32),
    }


def transform(vis, band_start):
    tick_moments = jnp.arange(SIDEREAL_TICKS, dtype=jnp.int32)
    azimuthal_orders = band_start[0] + jnp.arange(MBAND, dtype=jnp.int32)
    rotation_radians = azimuthal_orders[:, None] * tick_moments[None, :] % SIDEREAL_TICKS
    angle = rotation_radians.astype(jnp.float32) * (2.0 * math.pi / SIDEREAL_TICKS)
    trig_pair = jnp.concatenate([jnp.cos(angle), jnp.sin(angle)], 0)
    flat_visibility = vis.reshape(SIDEREAL_TICKS, 2 * BL)
    product = jnp.dot(trig_pair, flat_visibility, precision=lax.Precision.HIGHEST, preferred_element_type=jnp.float32)
    product = product.reshape(2, MBAND, 2, BL)
    scale = 1.0 / math.sqrt(SIDEREAL_TICKS)
    real_part = (product[0, :, 0] + product[1, :, 1]) * scale
    imag_part = (product[0, :, 1] - product[1, :, 0]) * scale
    return jnp.stack([real_part, imag_part], 1)

def one_mode(item):
    matrix, alm, spectrum = item
    wide = matrix.astype(jnp.float32)
    flat_matrix = wide.reshape(2 * BL, L)
    predicted = jnp.dot(flat_matrix, alm.astype(jnp.float32), precision=lax.Precision.HIGHEST).reshape(2, BL, 2)
    pred_real = predicted[0, :, 0] - predicted[1, :, 1]
    pred_imag = predicted[0, :, 1] + predicted[1, :, 0]
    resid_vis = (spectrum - jnp.stack([pred_real, pred_imag], 0)).astype(jnp.bfloat16)
    resid_vis = lax.optimization_barrier(resid_vis).astype(jnp.float32)
    columns = jnp.transpose(wide, (1, 0, 2)).reshape(BL, 2 * L)
    projected = jnp.dot(resid_vis, columns, precision=lax.Precision.HIGHEST).reshape(2, 2, L)
    alm_real = projected[0, 0] + projected[1, 1]
    alm_imag = projected[1, 0] - projected[0, 1]
    return jnp.stack([alm_real, alm_imag], 0)

def reference(vis, transfer, band_start, comp_index, comp_amp):
    spectra = transform(vis, band_start)
    summed = jax.ops.segment_sum(comp_amp, comp_index, num_segments=MBAND * L)
    model_alm = (summed.astype(jnp.float32) * (1.0 / 1024.0)).astype(jnp.bfloat16)
    model_alm = lax.optimization_barrier(model_alm).reshape(MBAND, L, 2)
    return lax.map(one_mode, (transfer, model_alm, spectra))
```

```python
import functools
import math

import jax
import jax.numpy as jnp
from jax import lax
from jax.experimental import pallas as pl
from jax.experimental.pallas import tpu as pltpu
from jax.sharding import PartitionSpec as P

LANES = 128
SPLIT = 64
UNIT = 1.0 / 1024.0


def padded(count, unit):
    return -(-count // unit) * unit


def cos_sin(phase, ticks):
    quarter = ticks // 4
    quadrant = (phase + quarter // 2) // quarter
    theta = (phase - quadrant * quarter).astype(jnp.float32) * (2.0 * math.pi / ticks)
    sq = theta * theta
    sine = theta * (1.0 + sq * (-1.0 / 6 + sq * (1.0 / 120 + sq * (-1.0 / 5040 + sq * (1.0 / 362880)))))
    cosine = 1.0 + sq * (-0.5 + sq * (1.0 / 24 + sq * (-1.0 / 720 + sq * (1.0 / 40320 - sq * (1.0 / 3628800)))))
    odd = (quadrant & 1) == 1
    cos_value = jnp.where(odd, sine, cosine)
    sin_value = jnp.where(odd, cosine, sine)
    cos_value = jnp.where(((quadrant + 1) & 2) == 2, -cos_value, cos_value)
    sin_value = jnp.where((quadrant & 2) == 2, -sin_value, sin_value)
    return cos_value, sin_value


def halves(value):
    high = value.astype(jnp.bfloat16)
    low = (value - high.astype(jnp.float32)).astype(jnp.bfloat16)
    return high, low


def transform_kernel(ticks, modes, m_local, comps, band_ref, vis_hbm, index_ref, amp_ref, out_ref, vis_ref, sem):
    copy = pltpu.make_async_copy(vis_hbm, vis_ref, sem)
    copy.start()
    rank = lax.axis_index("ma")
    devices = modes // m_local
    samples = ticks // devices
    pieces = vis_ref.shape[0] // samples
    tiles = pieces // 2
    order = band_ref[0] + lax.broadcasted_iota(jnp.int32, (modes, samples), 0)
    moment = rank * samples + lax.broadcasted_iota(jnp.int32, (modes, samples), 1)
    cos_value, sin_value = cos_sin((order * moment) % ticks, ticks)
    cos_high, cos_low = halves(cos_value)
    sin_high, sin_low = halves(sin_value)
    table = jnp.concatenate([cos_high, sin_high, cos_low, sin_low], 0)

    first = m_local * pieces
    chunks = padded(comps, LANES) // LANES
    for chunk in range(chunks):
        size = min(LANES, comps - chunk * LANES)
        for which in range(3):
            source = index_ref[...] if which == 0 else amp_ref[which - 1 : which, :]
            row = source[:, chunk * LANES : chunk * LANES + size].astype(jnp.float32)
            if size < LANES:
                row = jnp.concatenate([row, jnp.zeros((1, LANES - size), jnp.float32)], 1)
            out_ref[:, first + which * chunks + chunk, :] = jnp.broadcast_to(row, (devices, LANES))
    for spare in range(first + 3 * chunks, out_ref.shape[1]):
        out_ref[:, spare, :] = jnp.zeros((devices, LANES), jnp.float32)

    copy.wait()
    scale = 1.0 / math.sqrt(ticks)
    for tile in range(tiles):
        parts = [vis_ref[pl.ds(tile * 2 + part, samples, stride=pieces), :] for part in range(2)]
        high, low = halves(jnp.concatenate(parts, 1))
        product = jnp.dot(table, high, preferred_element_type=jnp.float32)
        product += jnp.dot(table, low, preferred_element_type=jnp.float32)
        product = product[: 2 * modes] + product[2 * modes :]
        from_cos, from_sin = product[:modes], product[modes:]
        real_part = (from_cos[:, :LANES] + from_sin[:, LANES:]) * scale
        imag_part = (from_cos[:, LANES:] - from_sin[:, :LANES]) * scale
        for local in range(m_local):
            rows = (local * pieces + tile, local * pieces + tiles + tile)
            if m_local == 1:
                out_ref[:, rows[0], :] = real_part
                out_ref[:, rows[1], :] = imag_part
            else:
                for device in range(devices):
                    mode = device * m_local + local
                    out_ref[device, rows[0] : rows[0] + 1, :] = real_part[mode : mode + 1]
                    out_ref[device, rows[1] : rows[1] + 1, :] = imag_part[mode : mode + 1]


def residual_kernel(m_local, pieces, chunks, got_ref, transfer_ref, out_ref):
    devices = got_ref.shape[0]
    baselines, width = transfer_ref.shape[2], transfer_ref.shape[3]
    tiles = pieces // 2
    groups = width // LANES
    base = lax.axis_index("ma") * (m_local * width)
    first = m_local * pieces
    spectra = got_ref[0]
    for device in range(1, devices):
        spectra += got_ref[device]

    def rows_of(which, chunk):
        return got_ref[:, first + which * chunks + chunk, :].astype(jnp.int32)

    offsets, amplitudes = [], []
    for chunk in range(chunks):
        offsets.append(rows_of(0, chunk) - base)
        amplitudes.append((rows_of(1, chunk), rows_of(2, chunk)))

    for local in range(m_local):
        selected, places = [], []
        for chunk in range(chunks):
            offset = offsets[chunk] - local * width
            group, place = offset // LANES, offset % LANES
            for device in range(devices):
                here = group[device : device + 1] == lax.broadcasted_iota(jnp.int32, (groups, LANES), 0)
                column = []
                for amplitude in amplitudes[chunk]:
                    value = amplitude[device : device + 1]
                    for part in (value // SPLIT, value % SPLIT):
                        column.append(jnp.where(here, part.astype(jnp.float32), 0.0))
                selected.append(jnp.concatenate(column, 0).astype(jnp.bfloat16))
                match = place[device : device + 1] == lax.broadcasted_iota(jnp.int32, (LANES, LANES), 0)
                places.append(jnp.where(match, 1.0, 0.0).astype(jnp.bfloat16))
        counted = lax.dot_general(
            jnp.concatenate(selected, 1),
            jnp.concatenate(places, 1),
            (((1,), (1,)), ((), ())),
            preferred_element_type=jnp.float32,
        ).astype(jnp.int32)
        model = []
        for part in range(2):
            high = counted[2 * part * groups : (2 * part + 1) * groups]
            low = counted[(2 * part + 1) * groups : (2 * part + 2) * groups]
            alm = (high * SPLIT + low).astype(jnp.float32) * UNIT
            model.append(jnp.concatenate([alm[g : g + 1] for g in range(groups)], 1))
        model_alm = jnp.concatenate(model, 0).astype(jnp.bfloat16)

        real_matrix, imag_matrix = transfer_ref[local, 0], transfer_ref[local, 1]
        contract = (((1,), (1,)), ((), ()))
        by_real = lax.dot_general(model_alm, real_matrix, contract, preferred_element_type=jnp.float32)
        by_imag = lax.dot_general(model_alm, imag_matrix, contract, preferred_element_type=jnp.float32)
        pred_real = by_real[0:1] - by_imag[1:2]
        pred_imag = by_real[1:2] + by_imag[0:1]
        start = local * pieces
        spectrum = [
            jnp.concatenate([spectra[start + part * tiles + t : start + part * tiles + t + 1] for t in range(tiles)], 1)
            for part in range(2)
        ]
        resid_real = (spectrum[0] - pred_real).astype(jnp.bfloat16)
        resid_imag = (spectrum[1] - pred_imag).astype(jnp.bfloat16)
        with_real = jnp.concatenate([resid_real, resid_imag], 0)
        with_imag = jnp.concatenate([resid_imag, -resid_real], 0)
        out_ref[local] = jnp.dot(with_real, real_matrix, preferred_element_type=jnp.float32) + jnp.dot(
            with_imag, imag_matrix, preferred_element_type=jnp.float32
        )


def body(vis, transfer, band_start, comp_index, comp_amp):
    devices = lax.axis_size("ma")
    samples, _, baselines = vis.shape
    m_local, _, _, width = transfer.shape
    comps = comp_index.shape[0]
    tiles = baselines // LANES
    pieces = 2 * tiles
    chunks = padded(comps, LANES) // LANES
    rows = padded(m_local * pieces + 3 * chunks, 8)
    vmem, smem = pl.BlockSpec(memory_space=pltpu.VMEM), pl.BlockSpec(memory_space=pltpu.SMEM)
    lines = vis.reshape(samples, 2, tiles, LANES).transpose(0, 2, 1, 3).reshape(samples * pieces, LANES)
    send = pl.pallas_call(
        functools.partial(transform_kernel, samples * devices, m_local * devices, m_local, comps),
        out_shape=jax.ShapeDtypeStruct((devices, rows, LANES), jnp.float32),
        in_specs=[smem, pl.BlockSpec(memory_space=pl.ANY), vmem, vmem],
        out_specs=vmem,
        scratch_shapes=[pltpu.VMEM((samples * pieces, LANES), jnp.float32), pltpu.SemaphoreType.DMA],
        name="transform",
    )(band_start, lines, comp_index.reshape(1, comps), comp_amp.T)
    got = lax.all_to_all(send, "ma", split_axis=0, concat_axis=0, tiled=True)
    return pl.pallas_call(
        functools.partial(residual_kernel, m_local, pieces, chunks),
        out_shape=jax.ShapeDtypeStruct((m_local, 2, width), jnp.float32),
        in_specs=[vmem, vmem],
        out_specs=vmem,
        name="residual",
    )(got, transfer)


def solution(mesh):
    in_specs = (
        P(("grp", "ma"), None, None),
        P(("grp", "ma"), None, None, None),
        P("grp"),
        P(("grp", "ma")),
        P(("grp", "ma"), None),
    )
    out_specs = P(("grp", "ma"), None, None)
    return jax.shard_map(body, mesh=mesh, in_specs=in_specs, out_specs=out_specs, check_vma=False)
```

```python
import functools
import math

import jax
import jax.numpy as jnp
from jax import lax
from jax.experimental import pallas as pl
from jax.experimental.pallas import tpu as pltpu
from jax.sharding import PartitionSpec as P

LANES = 128
SPLIT = 64
UNIT = 1.0 / 1024.0
VMEM_LIMIT = 32 * 2**20


def padded(count, unit):
    return -(-count // unit) * unit


def cos_sin(phase, ticks):
    quarter = ticks // 4
    quadrant = (phase + quarter // 2) // quarter
    theta = (phase - quadrant * quarter).astype(jnp.float32) * (2.0 * math.pi / ticks)
    sq = theta * theta
    sine = theta * (1.0 + sq * (-1.0 / 6 + sq * (1.0 / 120 + sq * (-1.0 / 5040 + sq * (1.0 / 362880)))))
    cosine = 1.0 + sq * (-0.5 + sq * (1.0 / 24 + sq * (-1.0 / 720 + sq * (1.0 / 40320 - sq * (1.0 / 3628800)))))
    odd = (quadrant & 1) == 1
    cos_value = jnp.where(odd, sine, cosine)
    sin_value = jnp.where(odd, cosine, sine)
    cos_value = jnp.where(((quadrant + 1) & 2) == 2, -cos_value, cos_value)
    sin_value = jnp.where((quadrant & 2) == 2, -sin_value, sin_value)
    return cos_value, sin_value


def halves(value):
    high = value.astype(jnp.bfloat16)
    low = (value - high.astype(jnp.float32)).astype(jnp.bfloat16)
    return high, low


def transform_kernel(ticks, modes, m_local, comps, *refs):
    band_ref, vis_hbm, index_hbm, amp_hbm, transfer_hbm, out_ref, transfer_ref, index_ref, amp_ref, vis_ref, sems = refs
    vis_copy = pltpu.make_async_copy(vis_hbm, vis_ref, sems.at[3])
    vis_copy.start()
    copies = [
        pltpu.make_async_copy(index_hbm, index_ref, sems.at[0]),
        pltpu.make_async_copy(amp_hbm, amp_ref, sems.at[1]),
        pltpu.make_async_copy(transfer_hbm, transfer_ref, sems.at[2]),
    ]
    for copy in copies:
        copy.start()
    rank = lax.axis_index("ma")
    devices = modes // m_local
    samples = ticks // devices
    pieces = vis_ref.shape[0] // samples
    tiles = pieces // 2
    order = band_ref[0] + lax.broadcasted_iota(jnp.int32, (modes, samples), 0)
    moment = rank * samples + lax.broadcasted_iota(jnp.int32, (modes, samples), 1)
    cos_value, sin_value = cos_sin((order * moment) % ticks, ticks)
    cos_high, cos_low = halves(cos_value)
    sin_high, sin_low = halves(sin_value)
    table = jnp.concatenate([cos_high, sin_high, cos_low, sin_low], 0)

    vis_copy.wait()
    scale = 1.0 / math.sqrt(ticks)
    for tile in range(tiles):
        parts = [vis_ref[pl.ds(tile * 2 + part, samples, stride=pieces), :] for part in range(2)]
        high, low = halves(jnp.concatenate(parts, 1))
        product = jnp.dot(table, high, preferred_element_type=jnp.float32)
        product += jnp.dot(table, low, preferred_element_type=jnp.float32)
        product = product[: 2 * modes] + product[2 * modes :]
        from_cos, from_sin = product[:modes], product[modes:]
        real_part = (from_cos[:, :LANES] + from_sin[:, LANES:]) * scale
        imag_part = (from_cos[:, LANES:] - from_sin[:, :LANES]) * scale
        for local in range(m_local):
            rows = (local * pieces + tile, local * pieces + tiles + tile)
            if m_local == 1:
                out_ref[:, rows[0], :] = real_part
                out_ref[:, rows[1], :] = imag_part
            else:
                for device in range(devices):
                    mode = device * m_local + local
                    out_ref[device, rows[0] : rows[0] + 1, :] = real_part[mode : mode + 1]
                    out_ref[device, rows[1] : rows[1] + 1, :] = imag_part[mode : mode + 1]

    first = m_local * pieces
    chunks = padded(comps, LANES) // LANES
    copies[0].wait()
    copies[1].wait()
    for chunk in range(chunks):
        size = min(LANES, comps - chunk * LANES)
        for which in range(3):
            source = index_ref[...] if which == 0 else amp_ref[which - 1 : which, :]
            row = source[:, chunk * LANES : chunk * LANES + size].astype(jnp.float32)
            if size < LANES:
                row = jnp.concatenate([row, jnp.zeros((1, LANES - size), jnp.float32)], 1)
            out_ref[:, first + which * chunks + chunk, :] = jnp.broadcast_to(row, (devices, LANES))
    for spare in range(first + 3 * chunks, out_ref.shape[1]):
        out_ref[:, spare, :] = jnp.zeros((devices, LANES), jnp.float32)
    copies[2].wait()


def residual_kernel(m_local, pieces, chunks, got_ref, transfer_ref, out_ref):
    devices = got_ref.shape[0]
    baselines, width = transfer_ref.shape[2], transfer_ref.shape[3]
    tiles = pieces // 2
    groups = width // LANES
    base = lax.axis_index("ma") * (m_local * width)
    first = m_local * pieces
    spectra = got_ref[0]
    for device in range(1, devices):
        spectra += got_ref[device]

    def rows_of(which, chunk):
        return got_ref[:, first + which * chunks + chunk, :].astype(jnp.int32)

    offsets, amplitudes = [], []
    for chunk in range(chunks):
        offsets.append(rows_of(0, chunk) - base)
        amplitudes.append((rows_of(1, chunk), rows_of(2, chunk)))

    for local in range(m_local):
        selected, places = [], []
        for chunk in range(chunks):
            offset = offsets[chunk] - local * width
            group, place = offset // LANES, offset % LANES
            for device in range(devices):
                here = group[device : device + 1] == lax.broadcasted_iota(jnp.int32, (groups, LANES), 0)
                column = []
                for amplitude in amplitudes[chunk]:
                    value = amplitude[device : device + 1]
                    for part in (value // SPLIT, value % SPLIT):
                        column.append(jnp.where(here, part.astype(jnp.float32), 0.0))
                selected.append(jnp.concatenate(column, 0).astype(jnp.bfloat16))
                match = place[device : device + 1] == lax.broadcasted_iota(jnp.int32, (LANES, LANES), 0)
                places.append(jnp.where(match, 1.0, 0.0).astype(jnp.bfloat16))
        counted = lax.dot_general(
            jnp.concatenate(selected, 1),
            jnp.concatenate(places, 1),
            (((1,), (1,)), ((), ())),
            preferred_element_type=jnp.float32,
        ).astype(jnp.int32)
        model = []
        for part in range(2):
            high = counted[2 * part * groups : (2 * part + 1) * groups]
            low = counted[(2 * part + 1) * groups : (2 * part + 2) * groups]
            alm = (high * SPLIT + low).astype(jnp.float32) * UNIT
            model.append(jnp.concatenate([alm[g : g + 1] for g in range(groups)], 1))
        model_alm = jnp.concatenate(model, 0).astype(jnp.bfloat16)

        real_matrix, imag_matrix = transfer_ref[local, 0], transfer_ref[local, 1]
        contract = (((1,), (1,)), ((), ()))
        by_real = lax.dot_general(model_alm, real_matrix, contract, preferred_element_type=jnp.float32)
        by_imag = lax.dot_general(model_alm, imag_matrix, contract, preferred_element_type=jnp.float32)
        pred_real = by_real[0:1] - by_imag[1:2]
        pred_imag = by_real[1:2] + by_imag[0:1]
        start = local * pieces
        spectrum = [
            jnp.concatenate([spectra[start + part * tiles + t : start + part * tiles + t + 1] for t in range(tiles)], 1)
            for part in range(2)
        ]
        resid_real = (spectrum[0] - pred_real).astype(jnp.bfloat16)
        resid_imag = (spectrum[1] - pred_imag).astype(jnp.bfloat16)
        with_real = jnp.concatenate([resid_real, resid_imag], 0)
        with_imag = jnp.concatenate([resid_imag, -resid_real], 0)
        out_ref[local] = jnp.dot(with_real, real_matrix, preferred_element_type=jnp.float32) + jnp.dot(
            with_imag, imag_matrix, preferred_element_type=jnp.float32
        )


def in_hbm(value):
    return pltpu.with_memory_space_constraint(value, pltpu.HBM)


def in_vmem(value):
    return pltpu.with_memory_space_constraint(value, pltpu.VMEM)


def body(vis, transfer, band_start, comp_index, comp_amp):
    devices = lax.axis_size("ma")
    samples, _, baselines = vis.shape
    m_local, _, _, width = transfer.shape
    comps = comp_index.shape[0]
    tiles = baselines // LANES
    pieces = 2 * tiles
    chunks = padded(comps, LANES) // LANES
    rows = padded(m_local * pieces + 3 * chunks, 8)
    vmem, smem, hbm = (pl.BlockSpec(memory_space=space) for space in (pltpu.VMEM, pltpu.SMEM, pltpu.HBM))
    lines = vis.reshape(samples, 2, tiles, LANES).transpose(0, 2, 1, 3).reshape(samples * pieces, LANES)
    send, matrices = pl.pallas_call(
        functools.partial(transform_kernel, samples * devices, m_local * devices, m_local, comps),
        out_shape=(pltpu.VMEM((devices, rows, LANES), jnp.float32), pltpu.VMEM(transfer.shape, transfer.dtype)),
        in_specs=[smem, hbm, hbm, hbm, hbm],
        out_specs=(vmem, vmem),
        scratch_shapes=[
            pltpu.VMEM((1, comps), jnp.int32),
            pltpu.VMEM((2, comps), jnp.int32),
            pltpu.VMEM(lines.shape, lines.dtype),
            pltpu.SemaphoreType.DMA((4,)),
        ],
        compiler_params=pltpu.CompilerParams(vmem_limit_bytes=VMEM_LIMIT),
        name="transform",
    )(band_start, in_hbm(lines), in_hbm(comp_index.reshape(1, comps)), in_hbm(comp_amp.T), in_hbm(transfer))
    got = lax.all_to_all(send, "ma", split_axis=0, concat_axis=0, tiled=True)
    return pl.pallas_call(
        functools.partial(residual_kernel, m_local, pieces, chunks),
        out_shape=jax.ShapeDtypeStruct((m_local, 2, width), jnp.float32),
        in_specs=[vmem, vmem],
        out_specs=vmem,
        compiler_params=pltpu.CompilerParams(vmem_limit_bytes=VMEM_LIMIT),
        name="residual",
    )(in_vmem(got), in_vmem(matrices))


def solution(mesh):
    in_specs = (
        P(("grp", "ma"), None, None),
        P(("grp", "ma"), None, None, None),
        P("grp"),
        P(("grp", "ma")),
        P(("grp", "ma"), None),
    )
    out_specs = P(("grp", "ma"), None, None)
    return jax.shard_map(body, mesh=mesh, in_specs=in_specs, out_specs=out_specs, check_vma=False)
```

```python
import functools
import math

import jax
import jax.numpy as jnp
from jax import lax
from jax.experimental import pallas as pl
from jax.experimental.pallas import tpu as pltpu
from jax.sharding import PartitionSpec as P

LANES = 128
SPLIT = 64
UNIT = 1.0 / 1024.0
VMEM_LIMIT = 32 * 2**20


def padded(count, unit):
    return -(-count // unit) * unit


def cos_sin(phase, ticks):
    quarter = ticks // 4
    quadrant = (phase + quarter // 2) // quarter
    theta = (phase - quadrant * quarter).astype(jnp.float32) * (2.0 * math.pi / ticks)
    sq = theta * theta
    sine = theta * (1.0 + sq * (-1.0 / 6 + sq * (1.0 / 120 + sq * (-1.0 / 5040 + sq * (1.0 / 362880)))))
    cosine = 1.0 + sq * (-0.5 + sq * (1.0 / 24 + sq * (-1.0 / 720 + sq * (1.0 / 40320 - sq * (1.0 / 3628800)))))
    odd = (quadrant & 1) == 1
    cos_value = jnp.where(odd, sine, cosine)
    sin_value = jnp.where(odd, cosine, sine)
    cos_value = jnp.where(((quadrant + 1) & 2) == 2, -cos_value, cos_value)
    sin_value = jnp.where((quadrant & 2) == 2, -sin_value, sin_value)
    return cos_value, sin_value


def halves(value):
    high = value.astype(jnp.bfloat16)
    low = (value - high.astype(jnp.float32)).astype(jnp.bfloat16)
    return high, low


def offsets_of(devices):
    return [1] + [step | 1 for step in (1 << bit for bit in range(1, devices.bit_length() - 1))]


def slot_size(comps):
    if comps >= LANES:
        return padded(comps, LANES)
    return 1 << (comps - 1).bit_length()


def transform_kernel(ticks, modes, m_local, comps, *refs):
    band_ref, vis_hbm, index_hbm, amp_hbm, transfer_hbm = refs[:5]
    send_ref, keep_ref, transfer_ref, index_ref, amp_ref, vis_ref, sems = refs[5:]
    vis_copy = pltpu.make_async_copy(vis_hbm, vis_ref, sems.at[3])
    vis_copy.start()
    copies = [
        pltpu.make_async_copy(index_hbm, index_ref, sems.at[0]),
        pltpu.make_async_copy(amp_hbm, amp_ref, sems.at[1]),
        pltpu.make_async_copy(transfer_hbm, transfer_ref, sems.at[2]),
    ]
    for copy in copies:
        copy.start()
    rank = lax.axis_index("ma")
    devices = modes // m_local
    samples = ticks // devices
    pieces = vis_ref.shape[0] // samples
    tiles = pieces // 2
    row = lax.broadcasted_iota(jnp.int32, (modes, samples), 0)
    position = row % devices
    receiver = jnp.broadcast_to(rank, (modes, samples))
    for step, offset in enumerate(offsets_of(devices)):
        receiver ^= jnp.where((position & (devices >> (step + 1))) == 0, offset, 0)
    order = band_ref[0] + receiver * m_local + row // devices
    moment = rank * samples + lax.broadcasted_iota(jnp.int32, (modes, samples), 1)
    cos_value, sin_value = cos_sin((order * moment) % ticks, ticks)
    cos_high, cos_low = halves(cos_value)
    sin_high, sin_low = halves(sin_value)
    table = jnp.concatenate([cos_high, sin_high, cos_low, sin_low], 0)

    half, size = devices // 2, m_local * pieces
    first = send_ref.shape[0] - half * size
    vis_copy.wait()
    scale = 1.0 / math.sqrt(ticks)
    for tile in range(tiles):
        parts = [vis_ref[pl.ds(tile * 2 + part, samples, stride=pieces), :] for part in range(2)]
        high, low = halves(jnp.concatenate(parts, 1))
        product = jnp.dot(table, high, preferred_element_type=jnp.float32)
        product += jnp.dot(table, low, preferred_element_type=jnp.float32)
        product = product[: 2 * modes] + product[2 * modes :]
        from_cos, from_sin = product[:modes], product[modes:]
        real_part = (from_cos[:, :LANES] + from_sin[:, LANES:]) * scale
        imag_part = (from_cos[:, LANES:] - from_sin[:, :LANES]) * scale
        for local in range(m_local):
            for part, value in enumerate((real_part, imag_part)):
                start = first + local * pieces + part * tiles + tile
                at = local * devices
                send_ref[pl.ds(start, half, stride=size), :] = value[at : at + half]
                keep_ref[pl.ds(start, half, stride=size), :] = value[at + half : at + devices]

    slot = slot_size(comps)
    lines = max(1, slot // LANES)
    width = slot // lines
    send_ref[:first] = jnp.zeros((first, LANES), jnp.float32)
    keep_ref[:first] = jnp.zeros((first, LANES), jnp.float32)
    copies[0].wait()
    copies[1].wait()
    lane = lax.broadcasted_iota(jnp.int32, (1, LANES), 1)
    mine = lane // width == rank % (LANES // width)
    for which in range(3):
        source = index_ref[...] if which == 0 else amp_ref[which - 1 : which, :]
        for line in range(lines):
            value = source[:, line * width : (line + 1) * width].astype(jnp.float32)
            if value.shape[1] < width:
                value = jnp.concatenate([value, jnp.zeros((1, width - value.shape[1]), jnp.float32)], 1)
            value = jnp.where(mine, jnp.concatenate([value] * (LANES // width), 1), 0.0)
            at = which * (first // 3) + rank * slot // LANES + line
            send_ref[pl.ds(at, 1), :] = value
            keep_ref[pl.ds(at, 1), :] = value
    copies[2].wait()


def residual_kernel(m_local, pieces, held_ref, got_ref, transfer_ref, out_ref):
    width = transfer_ref.shape[3]
    tiles = pieces // 2
    groups = width // LANES
    base = lax.axis_index("ma") * (m_local * width)
    size = m_local * pieces
    first = got_ref.shape[0] - size
    count = first // 3
    shift = held_ref.shape[0] - got_ref.shape[0]
    components = (held_ref[:first] + got_ref[:first]).astype(jnp.int32)
    spectra = held_ref[first + shift :] + got_ref[first:]
    offsets = components[:count] - base
    amplitudes = (components[count : 2 * count], components[2 * count :])

    for local in range(m_local):
        offset = offsets - local * width
        group, place = offset // LANES, offset % LANES
        selected, places = [], []
        for line in range(count):
            here = group[line : line + 1] == lax.broadcasted_iota(jnp.int32, (groups, LANES), 0)
            column = []
            for amplitude in amplitudes:
                value = amplitude[line : line + 1]
                for part in (value // SPLIT, value % SPLIT):
                    column.append(jnp.where(here, part.astype(jnp.float32), 0.0))
            selected.append(jnp.concatenate(column, 0).astype(jnp.bfloat16))
            match = place[line : line + 1] == lax.broadcasted_iota(jnp.int32, (LANES, LANES), 0)
            places.append(jnp.where(match, 1.0, 0.0).astype(jnp.bfloat16))
        contract = (((1,), (1,)), ((), ()))
        counted = lax.dot_general(
            jnp.concatenate(selected, 1),
            jnp.concatenate(places, 1),
            contract,
            preferred_element_type=jnp.float32,
        ).astype(jnp.int32)
        model = []
        for part in range(2):
            high = counted[2 * part * groups : (2 * part + 1) * groups]
            low = counted[(2 * part + 1) * groups : (2 * part + 2) * groups]
            alm = (high * SPLIT + low).astype(jnp.float32) * UNIT
            model.append(jnp.concatenate([alm[g : g + 1] for g in range(groups)], 1))
        model_alm = jnp.concatenate(model, 0).astype(jnp.bfloat16)

        real_matrix, imag_matrix = transfer_ref[local, 0], transfer_ref[local, 1]
        by_real = lax.dot_general(model_alm, real_matrix, contract, preferred_element_type=jnp.float32)
        by_imag = lax.dot_general(model_alm, imag_matrix, contract, preferred_element_type=jnp.float32)
        pred_real = by_real[0:1] - by_imag[1:2]
        pred_imag = by_real[1:2] + by_imag[0:1]
        start = local * pieces
        spectrum = [
            jnp.concatenate([spectra[start + part * tiles + t : start + part * tiles + t + 1] for t in range(tiles)], 1)
            for part in range(2)
        ]
        resid_real = (spectrum[0] - pred_real).astype(jnp.bfloat16)
        resid_imag = (spectrum[1] - pred_imag).astype(jnp.bfloat16)
        with_real = jnp.concatenate([resid_real, resid_imag], 0)
        with_imag = jnp.concatenate([resid_imag, -resid_real], 0)
        out_ref[local] = jnp.dot(with_real, real_matrix, preferred_element_type=jnp.float32) + jnp.dot(
            with_imag, imag_matrix, preferred_element_type=jnp.float32
        )


def in_hbm(value):
    return pltpu.with_memory_space_constraint(value, pltpu.HBM)


def in_vmem(value):
    return pltpu.with_memory_space_constraint(value, pltpu.VMEM)


def swap(value, offset, devices):
    return lax.ppermute(value, "ma", [(device, device ^ offset) for device in range(devices)])


def body(vis, transfer, band_start, comp_index, comp_amp):
    devices = lax.axis_size("ma")
    samples, _, baselines = vis.shape
    m_local, _, _, width = transfer.shape
    comps = comp_index.shape[0]
    tiles = baselines // LANES
    pieces = 2 * tiles
    size = m_local * pieces
    first = 3 * padded(devices * slot_size(comps), LANES) // LANES
    rows = first + devices // 2 * size
    vmem, smem, hbm = (pl.BlockSpec(memory_space=space) for space in (pltpu.VMEM, pltpu.SMEM, pltpu.HBM))
    lines = vis.reshape(samples, 2, tiles, LANES).transpose(0, 2, 1, 3).reshape(samples * pieces, LANES)
    block = pltpu.VMEM((rows, LANES), jnp.float32)
    send, held, matrices = pl.pallas_call(
        functools.partial(transform_kernel, samples * devices, m_local * devices, m_local, comps),
        out_shape=(block, block, pltpu.VMEM(transfer.shape, transfer.dtype)),
        in_specs=[smem, hbm, hbm, hbm, hbm],
        out_specs=(vmem, vmem, vmem),
        scratch_shapes=[
            pltpu.VMEM((1, comps), jnp.int32),
            pltpu.VMEM((2, comps), jnp.int32),
            pltpu.VMEM(lines.shape, lines.dtype),
            pltpu.SemaphoreType.DMA((4,)),
        ],
        compiler_params=pltpu.CompilerParams(vmem_limit_bytes=VMEM_LIMIT),
        name="transform",
    )(band_start, in_hbm(lines), in_hbm(comp_index.reshape(1, comps)), in_hbm(comp_amp.T), in_hbm(transfer))
    offsets = offsets_of(devices)
    got = swap(send, offsets[0], devices)
    for step, offset in enumerate(offsets[1:], 1):
        shift = held.shape[0] - got.shape[0]
        summed = jnp.concatenate([held[:first] + got[:first], held[first + shift :] + got[first:]], 0)
        rows = first + (devices >> (step + 1)) * size
        held, got = summed, swap(summed[:rows], offset, devices)
    return pl.pallas_call(
        functools.partial(residual_kernel, m_local, pieces),
        out_shape=jax.ShapeDtypeStruct((m_local, 2, width), jnp.float32),
        in_specs=[vmem, vmem, vmem],
        out_specs=vmem,
        compiler_params=pltpu.CompilerParams(vmem_limit_bytes=VMEM_LIMIT),
        name="residual",
    )(in_vmem(held), in_vmem(got), in_vmem(matrices))


def solution(mesh):
    in_specs = (
        P(("grp", "ma"), None, None),
        P(("grp", "ma"), None, None, None),
        P("grp"),
        P(("grp", "ma")),
        P(("grp", "ma"), None),
    )
    out_specs = P(("grp", "ma"), None, None)
    return jax.shard_map(body, mesh=mesh, in_specs=in_specs, out_specs=out_specs, check_vma=False)
```

```python
import functools
import math

import jax
import jax.numpy as jnp
from jax import lax
from jax.experimental import pallas as pl
from jax.experimental.pallas import tpu as pltpu
from jax.sharding import PartitionSpec as P

LANE_BITS = 7
LANES = 1 << LANE_BITS
SPLIT_BITS = 6
SPLIT = 1 << SPLIT_BITS
NT = (((1,), (1,)), ((), ()))
BLOCK = 256
UNIT = 1.0 / 1024.0
VMEM_LIMIT = 32 * 2**20
LEAD = 4 * 10**8


def padded(count, unit):
    return -(-count // unit) * unit


def cos_sin(phase, ticks):
    quarter = ticks // 4
    quadrant = (phase + quarter // 2) >> (quarter.bit_length() - 1)
    theta = (phase - quadrant * quarter).astype(jnp.float32) * (2.0 * math.pi / ticks)
    sq = theta * theta
    sine = theta * (1.0 + sq * (-1.0 / 6 + sq * (1.0 / 120 + sq * (-1.0 / 5040 + sq * (1.0 / 362880)))))
    cosine = 1.0 + sq * (-0.5 + sq * (1.0 / 24 + sq * (-1.0 / 720 + sq * (1.0 / 40320 - sq * (1.0 / 3628800)))))
    odd = (quadrant & 1) == 1
    cos_value = jnp.where(odd, sine, cosine)
    sin_value = jnp.where(odd, cosine, sine)
    cos_value = jnp.where(((quadrant + 1) & 2) == 2, -cos_value, cos_value)
    sin_value = jnp.where((quadrant & 2) == 2, -sin_value, sin_value)
    return cos_value, sin_value


def halves(value):
    high = value.astype(jnp.bfloat16)
    low = (value - high.astype(jnp.float32)).astype(jnp.bfloat16)
    return high, low


def offsets_of(devices):
    return [1] + [step | 1 for step in (1 << bit for bit in range(1, devices.bit_length() - 1))]


def tile_of(comps):
    lanes = LANES // 2 if comps <= LANES // 2 else LANES
    lines = -(-comps // lanes)
    parts = 4 * lanes // LANES
    return lanes, lines, parts, padded(3 * lines * parts, 8)


def table_kernel(ticks, m_local, *refs):
    band_ref, index_hbm, amp_hbm, table_ref, own_ref, index_ref, amp_ref, sems = refs
    copies = [
        pltpu.make_async_copy(index_hbm, index_ref, sems.at[0]),
        pltpu.make_async_copy(amp_hbm, amp_ref, sems.at[1]),
    ]
    for copy in copies:
        copy.start()
    rank = lax.axis_index("ma")
    modes, samples = table_ref.shape[0] // 4, table_ref.shape[1]
    devices = modes // m_local
    row = lax.broadcasted_iota(jnp.int32, (modes, samples), 0)
    position = row % devices
    receiver = jnp.broadcast_to(rank, (modes, samples))
    for step, offset in enumerate(offsets_of(devices)):
        receiver ^= jnp.where((position & (devices >> (step + 1))) == 0, offset, 0)
    order = band_ref[0] + receiver * m_local + row // devices
    moment = rank * samples + lax.broadcasted_iota(jnp.int32, (modes, samples), 1)
    values = [halves(value) for value in cos_sin((order * moment) & (ticks - 1), ticks)]
    for part in range(4):
        table_ref[part * modes : (part + 1) * modes] = values[part % 2][part // 2]

    comps = index_ref.shape[1]
    lanes, lines, parts, _ = tile_of(comps)
    own_ref[...] = jnp.zeros(own_ref.shape, jnp.float32)
    shared = LANES // lanes
    mine = lax.broadcasted_iota(jnp.int32, (1, LANES), 1) // lanes == rank % shared
    start = 3 * lines * (rank % 4 // shared)
    for copy in copies:
        copy.wait()
    for which in range(3):
        source = index_ref[...] if which == 0 else amp_ref[which - 1 : which, :]
        for line in range(lines):
            value = source[:, line * lanes : (line + 1) * lanes].astype(jnp.float32)
            if value.shape[1] < lanes:
                value = jnp.concatenate([value, jnp.zeros((1, lanes - value.shape[1]), jnp.float32)], 1)
            value = jnp.where(mine, jnp.concatenate([value] * shared, 1), 0.0)
            own_ref[pl.ds(start + which * lines + line, 1), :] = value


def transform_kernel(ticks, m_local, table_ref, vis_ref, own_ref, send_ref, keep_ref):
    modes, samples = table_ref.shape[0] // 4, table_ref.shape[1]
    devices = modes // m_local
    pieces = vis_ref.shape[0] // samples
    tiles = pieces // 2
    half, size = devices // 2, m_local * pieces
    first = own_ref.shape[0]
    send_ref[:first] = own_ref[...]
    keep_ref[:first] = own_ref[...]
    scale = 1.0 / math.sqrt(ticks)
    for tile in range(tiles):
        parts = [vis_ref[pl.ds(tile * 2 + part, samples, stride=pieces), :] for part in range(2)]
        high, low = halves(jnp.concatenate(parts, 1))
        product = jnp.dot(table_ref[...], high, preferred_element_type=jnp.float32)
        product += jnp.dot(table_ref[...], low, preferred_element_type=jnp.float32)
        product = product[: 2 * modes] + product[2 * modes :]
        from_cos, from_sin = product[:modes], product[modes:]
        real_part = (from_cos[:, :LANES] + from_sin[:, LANES:]) * scale
        imag_part = (from_cos[:, LANES:] - from_sin[:, :LANES]) * scale
        for local in range(m_local):
            for part, value in enumerate((real_part, imag_part)):
                start = first + local * pieces + part * tiles + tile
                at = local * devices
                send_ref[pl.ds(start, half, stride=size), :] = value[at : at + half]
                keep_ref[pl.ds(start, half, stride=size), :] = value[at + half : at + devices]


def fetch_kernel(after_ref, transfer_hbm, transfer_ref, sem):
    copy = pltpu.make_async_copy(transfer_hbm, transfer_ref, sem)
    copy.start()
    copy.wait()


def counts_of(components, comps, base, groups):
    lanes, lines, parts, rows = tile_of(comps)
    numbers = components.astype(jnp.int32)
    group, place = (numbers - base) >> LANE_BITS, (numbers - base) & (LANES - 1)
    high, low = (numbers >> SPLIT_BITS).astype(jnp.float32), (numbers & (SPLIT - 1)).astype(jnp.float32)
    slot = lax.broadcasted_iota(jnp.int32, (groups, LANES), 0)
    lane = lax.broadcasted_iota(jnp.int32, (LANES, LANES), 0)
    selected, places = [], []
    for tile in range(components.shape[0] // rows):
        for part in range(parts):
            for line in range(lines):
                at = tile * rows + 3 * lines * part + line
                here = group[at : at + 1] == slot
                column = []
                for field in (at + lines, at + 2 * lines):
                    column += [jnp.where(here, value[field : field + 1], 0.0) for value in (high, low)]
                selected.append(jnp.concatenate(column, 0).astype(jnp.bfloat16))
                places.append(jnp.where(place[at : at + 1] == lane, 1.0, 0.0).astype(jnp.bfloat16))
    return lax.dot_general(
        jnp.concatenate(selected, 1), jnp.concatenate(places, 1), NT, preferred_element_type=jnp.float32
    )


def count_kernel(m_local, width, comps, held_ref, count_ref):
    groups = width // LANES
    first = held_ref.shape[0]
    for local in range(m_local):
        base = (lax.axis_index("ma") * m_local + local) * width
        count_ref[local] = counts_of(held_ref[...], comps, base, groups)


def residual_kernel(m_local, pieces, comps, count_ref, held_ref, got_ref, transfer_ref, out_ref):
    width = transfer_ref.shape[3]
    tiles = pieces // 2
    groups = width // LANES
    size = m_local * pieces
    first = got_ref.shape[0] - size
    spectra = held_ref[...] + got_ref[first:]
    for local in range(m_local):
        base = (lax.axis_index("ma") * m_local + local) * width
        counted = (count_ref[local] + counts_of(got_ref[:first], comps, base, groups)).astype(jnp.int32)
        model = []
        for part in range(2):
            high = counted[2 * part * groups : (2 * part + 1) * groups]
            low = counted[(2 * part + 1) * groups : (2 * part + 2) * groups]
            alm = ((high << SPLIT_BITS) + low).astype(jnp.float32) * UNIT
            model.append(jnp.concatenate([alm[g : g + 1] for g in range(groups)], 1))
        model_alm = jnp.concatenate(model, 0).astype(jnp.bfloat16)

        real_matrix, imag_matrix = transfer_ref[local, 0], transfer_ref[local, 1]
        by_real = lax.dot_general(model_alm, real_matrix, NT, preferred_element_type=jnp.float32)
        by_imag = lax.dot_general(model_alm, imag_matrix, NT, preferred_element_type=jnp.float32)
        pred_real = by_real[0:1] - by_imag[1:2]
        pred_imag = by_real[1:2] + by_imag[0:1]
        start = local * pieces
        spectrum = [
            jnp.concatenate([spectra[start + part * tiles + t : start + part * tiles + t + 1] for t in range(tiles)], 1)
            for part in range(2)
        ]
        resid_real = (spectrum[0] - pred_real).astype(jnp.bfloat16)
        resid_imag = (spectrum[1] - pred_imag).astype(jnp.bfloat16)
        with_real = jnp.concatenate([resid_real, resid_imag], 0)
        with_imag = jnp.concatenate([resid_imag, -resid_real], 0)
        for column in range(0, width, BLOCK):
            block = slice(column, column + BLOCK)
            out_ref[local, :, block] = jnp.dot(
                with_real, real_matrix[:, block], preferred_element_type=jnp.float32
            ) + jnp.dot(with_imag, imag_matrix[:, block], preferred_element_type=jnp.float32)


def in_hbm(value):
    return pltpu.with_memory_space_constraint(value, pltpu.HBM)


def in_vmem(value):
    return pltpu.with_memory_space_constraint(value, pltpu.VMEM)


def swap(value, offset, devices):
    return lax.ppermute(value, "ma", [(device, device ^ offset) for device in range(devices)])


def body(vis, transfer, band_start, comp_index, comp_amp):
    devices = lax.axis_size("ma")
    samples, _, baselines = vis.shape
    m_local, _, _, width = transfer.shape
    comps = comp_index.shape[0]
    tiles = baselines // LANES
    pieces = 2 * tiles
    size = m_local * pieces
    unit = tile_of(comps)[3]
    vmem, smem, hbm = (pl.BlockSpec(memory_space=space) for space in (pltpu.VMEM, pltpu.SMEM, pltpu.HBM))
    params = pltpu.CompilerParams(vmem_limit_bytes=VMEM_LIMIT)
    lines = vis.reshape(samples, 2, tiles, LANES).transpose(0, 2, 1, 3).reshape(samples * pieces, LANES)
    table, own = pl.pallas_call(
        functools.partial(table_kernel, samples * devices, m_local),
        out_shape=(
            pltpu.VMEM((4 * m_local * devices, samples), jnp.bfloat16),
            pltpu.VMEM((unit, LANES), jnp.float32),
        ),
        in_specs=[smem, hbm, hbm],
        out_specs=(vmem, vmem),
        scratch_shapes=[
            pltpu.VMEM((1, comps), jnp.int32),
            pltpu.VMEM((2, comps), jnp.int32),
            pltpu.SemaphoreType.DMA((2,)),
        ],
        compiler_params=params,
        cost_estimate=pl.CostEstimate(flops=LEAD, transcendentals=0, bytes_accessed=0),
        name="table",
    )(band_start, in_hbm(comp_index.reshape(1, comps)), in_hbm(comp_amp.T))
    part = pltpu.VMEM((unit + devices // 2 * size, LANES), jnp.float32)
    send, keep = pl.pallas_call(
        functools.partial(transform_kernel, samples * devices, m_local),
        out_shape=(part, part),
        in_specs=[vmem, vmem, vmem],
        out_specs=(vmem, vmem),
        compiler_params=params,
        name="transform",
    )(in_vmem(table), in_vmem(lines), in_vmem(own))
    offsets = offsets_of(devices)
    got = swap(send, offsets[0], devices)
    components, spectra = keep[:unit], keep[unit:]
    for step, offset in enumerate(offsets[1:], 1):
        first = got.shape[0] - spectra.shape[0]
        if step <= 2:
            components = components + got[:first]
        else:
            components = jnp.concatenate([components, got[:first]], 0)
        spectra = spectra + got[first:]
        going = spectra.shape[0] // 2
        send = jnp.concatenate([components, spectra[:going]], 0)
        if step == 1:
            matrices = pl.pallas_call(
                fetch_kernel,
                out_shape=pltpu.VMEM(transfer.shape, transfer.dtype),
                in_specs=[vmem, hbm],
                out_specs=vmem,
                scratch_shapes=[pltpu.SemaphoreType.DMA],
                compiler_params=params,
                name="fetch",
            )(in_vmem(send), in_hbm(transfer))
        got, spectra = swap(send, offset, devices), spectra[going:]
    count = pl.pallas_call(
        functools.partial(count_kernel, m_local, width, comps),
        out_shape=pltpu.VMEM((m_local, 4 * width // LANES, LANES), jnp.float32),
        in_specs=[vmem],
        out_specs=vmem,
        compiler_params=params,
        name="count",
    )(in_vmem(components))
    return pl.pallas_call(
        functools.partial(residual_kernel, m_local, pieces, comps),
        out_shape=jax.ShapeDtypeStruct((m_local, 2, width), jnp.float32),
        in_specs=[vmem, vmem, vmem, vmem],
        out_specs=vmem,
        compiler_params=params,
        name="residual",
    )(in_vmem(count), in_vmem(spectra), in_vmem(got), in_vmem(matrices))


def solution(mesh):
    in_specs = (
        P(("grp", "ma"), None, None),
        P(("grp", "ma"), None, None, None),
        P("grp"),
        P(("grp", "ma")),
        P(("grp", "ma"), None),
    )
    out_specs = P(("grp", "ma"), None, None)
    return jax.shard_map(body, mesh=mesh, in_specs=in_specs, out_specs=out_specs, check_vma=False)
```

```python
import functools
import math

import jax
import jax.numpy as jnp
from jax import lax
from jax.experimental import pallas as pl
from jax.experimental.pallas import tpu as pltpu
from jax.sharding import PartitionSpec as P

LANE_BITS = 7
LANES = 1 << LANE_BITS
SPLIT_BITS = 6
SPLIT = 1 << SPLIT_BITS
NT = (((1,), (1,)), ((), ()))
BLOCK = 256
UNIT = 1.0 / 1024.0
VMEM_LIMIT = 32 * 2**20
LEAD = 400000000


def padded(count, unit):
    return -(-count // unit) * unit


def cos_sin(phase, ticks):
    quarter = ticks // 4
    quadrant = (phase + quarter // 2) >> (quarter.bit_length() - 1)
    theta = (phase - quadrant * quarter).astype(jnp.float32) * (2.0 * math.pi / ticks)
    sq = theta * theta
    sine = theta * (1.0 + sq * (-1.0 / 6 + sq * (1.0 / 120 + sq * (-1.0 / 5040 + sq * (1.0 / 362880)))))
    cosine = 1.0 + sq * (-0.5 + sq * (1.0 / 24 + sq * (-1.0 / 720 + sq * (1.0 / 40320 - sq * (1.0 / 3628800)))))
    odd = (quadrant & 1) == 1
    cos_value = jnp.where(odd, sine, cosine)
    sin_value = jnp.where(odd, cosine, sine)
    cos_value = jnp.where(((quadrant + 1) & 2) == 2, -cos_value, cos_value)
    sin_value = jnp.where((quadrant & 2) == 2, -sin_value, sin_value)
    return cos_value, sin_value


def halves(value):
    high = value.astype(jnp.bfloat16)
    low = (value - high.astype(jnp.float32)).astype(jnp.bfloat16)
    return high, low


def offsets_of(devices):
    return [1] + [step | 1 for step in (1 << bit for bit in range(1, devices.bit_length() - 1))]


def tile_of(comps):
    lanes = LANES // 2 if comps <= LANES // 2 else LANES
    lines = -(-comps // lanes)
    parts = 4 * lanes // LANES
    return lanes, lines, parts, padded(3 * lines * parts, 8)


def table_kernel(ticks, m_local, band_ref, table_ref):
    rank = lax.axis_index("ma")
    modes, samples = table_ref.shape[0] // 4, table_ref.shape[1]
    devices = modes // m_local
    row = lax.broadcasted_iota(jnp.int32, (modes, samples), 0)
    position = row % devices
    receiver = jnp.broadcast_to(rank, (modes, samples))
    for step, offset in enumerate(offsets_of(devices)):
        receiver ^= jnp.where((position & (devices >> (step + 1))) == 0, offset, 0)
    order = band_ref[0] + receiver * m_local + row // devices
    moment = rank * samples + lax.broadcasted_iota(jnp.int32, (modes, samples), 1)
    values = [halves(value) for value in cos_sin((order * moment) & (ticks - 1), ticks)]
    for part in range(4):
        table_ref[part * modes : (part + 1) * modes] = values[part % 2][part // 2]


def pack_kernel(after_ref, index_hbm, amp_hbm, index_other_ref, amp_other_ref, tile_ref, index_ref, amp_ref, sems):
    copies = [
        pltpu.make_async_copy(index_hbm, index_ref, sems.at[0]),
        pltpu.make_async_copy(amp_hbm, amp_ref, sems.at[1]),
    ]
    for copy in copies:
        copy.start()
    comps = index_ref.shape[1]
    lanes, lines, _, _ = tile_of(comps)
    shared = LANES // lanes
    tile_ref[...] = jnp.zeros(tile_ref.shape, jnp.float32)
    for copy in copies:
        copy.wait()
    lane = lax.broadcasted_iota(jnp.int32, (1, LANES), 1) // lanes
    own = lax.axis_index("ma")
    other = own ^ 1
    for which in range(3):
        for line in range(lines):
            rows = []
            for index, amp in ((index_ref, amp_ref), (index_other_ref, amp_other_ref)):
                source = index[...] if which == 0 else amp[which - 1 : which, :]
                value = source[:, line * lanes : (line + 1) * lanes].astype(jnp.float32)
                if value.shape[1] < lanes:
                    value = jnp.concatenate([value, jnp.zeros((1, lanes - value.shape[1]), jnp.float32)], 1)
                rows.append(jnp.concatenate([value] * shared, 1))
            place = which * lines + line
            if shared == 2:
                value = jnp.where(lane == own % 2, rows[0], rows[1])
                tile_ref[pl.ds(3 * lines * (own % 4 // 2) + place, 1), :] = value
            else:
                tile_ref[pl.ds(3 * lines * (own % 4) + place, 1), :] = rows[0]
                tile_ref[pl.ds(3 * lines * (other % 4) + place, 1), :] = rows[1]


def transform_kernel(ticks, m_local, table_ref, vis_ref, send_ref, keep_ref):
    modes, samples = table_ref.shape[0] // 4, table_ref.shape[1]
    devices = modes // m_local
    pieces = vis_ref.shape[0] // samples
    tiles = pieces // 2
    half, size = devices // 2, m_local * pieces
    scale = 1.0 / math.sqrt(ticks)
    for tile in range(tiles):
        parts = [vis_ref[pl.ds(tile * 2 + part, samples, stride=pieces), :] for part in range(2)]
        high, low = halves(jnp.concatenate(parts, 1))
        product = jnp.dot(table_ref[...], high, preferred_element_type=jnp.float32)
        product += jnp.dot(table_ref[...], low, preferred_element_type=jnp.float32)
        product = product[: 2 * modes] + product[2 * modes :]
        from_cos, from_sin = product[:modes], product[modes:]
        real_part = (from_cos[:, :LANES] + from_sin[:, LANES:]) * scale
        imag_part = (from_cos[:, LANES:] - from_sin[:, :LANES]) * scale
        for local in range(m_local):
            for part, value in enumerate((real_part, imag_part)):
                start = local * pieces + part * tiles + tile
                at = local * devices
                send_ref[pl.ds(start, half, stride=size), :] = value[at : at + half]
                keep_ref[pl.ds(start, half, stride=size), :] = value[at + half : at + devices]


def fetch_kernel(after_ref, transfer_hbm, transfer_ref, sem):
    copy = pltpu.make_async_copy(transfer_hbm, transfer_ref, sem)
    copy.start()
    copy.wait()


def counts_of(components, comps, base, groups):
    _, lines, parts, rows = tile_of(comps)
    numbers = components.astype(jnp.int32)
    group, place = (numbers - base) >> LANE_BITS, (numbers - base) & (LANES - 1)
    high, low = (numbers >> SPLIT_BITS).astype(jnp.float32), (numbers & (SPLIT - 1)).astype(jnp.float32)
    slot = lax.broadcasted_iota(jnp.int32, (groups, LANES), 0)
    lane = lax.broadcasted_iota(jnp.int32, (LANES, LANES), 0)
    selected, places = [], []
    for tile in range(components.shape[0] // rows):
        for part in range(parts):
            for line in range(lines):
                at = tile * rows + 3 * lines * part + line
                here = group[at : at + 1] == slot
                column = []
                for field in (at + lines, at + 2 * lines):
                    column += [jnp.where(here, value[field : field + 1], 0.0) for value in (high, low)]
                selected.append(jnp.concatenate(column, 0).astype(jnp.bfloat16))
                places.append(jnp.where(place[at : at + 1] == lane, 1.0, 0.0).astype(jnp.bfloat16))
    return lax.dot_general(
        jnp.concatenate(selected, 1), jnp.concatenate(places, 1), NT, preferred_element_type=jnp.float32
    )


def count_kernel(m_local, width, comps, held_ref, count_ref):
    groups = width // LANES
    for local in range(m_local):
        base = (lax.axis_index("ma") * m_local + local) * width
        count_ref[local] = counts_of(held_ref[...], comps, base, groups)


def residual_kernel(m_local, pieces, comps, count_ref, held_ref, got_ref, transfer_ref, out_ref):
    width = transfer_ref.shape[3]
    tiles = pieces // 2
    groups = width // LANES
    size = m_local * pieces
    first = got_ref.shape[0] - size
    spectra = held_ref[...] + got_ref[first:]
    for local in range(m_local):
        base = (lax.axis_index("ma") * m_local + local) * width
        counted = (count_ref[local] + counts_of(got_ref[:first], comps, base, groups)).astype(jnp.int32)
        model = []
        for part in range(2):
            high = counted[2 * part * groups : (2 * part + 1) * groups]
            low = counted[(2 * part + 1) * groups : (2 * part + 2) * groups]
            alm = ((high << SPLIT_BITS) + low).astype(jnp.float32) * UNIT
            model.append(jnp.concatenate([alm[g : g + 1] for g in range(groups)], 1))
        model_alm = jnp.concatenate(model, 0).astype(jnp.bfloat16)

        real_matrix, imag_matrix = transfer_ref[local, 0], transfer_ref[local, 1]
        by_real = lax.dot_general(model_alm, real_matrix, NT, preferred_element_type=jnp.float32)
        by_imag = lax.dot_general(model_alm, imag_matrix, NT, preferred_element_type=jnp.float32)
        pred_real = by_real[0:1] - by_imag[1:2]
        pred_imag = by_real[1:2] + by_imag[0:1]
        start = local * pieces
        spectrum = [
            jnp.concatenate([spectra[start + part * tiles + t : start + part * tiles + t + 1] for t in range(tiles)], 1)
            for part in range(2)
        ]
        resid_real = (spectrum[0] - pred_real).astype(jnp.bfloat16)
        resid_imag = (spectrum[1] - pred_imag).astype(jnp.bfloat16)
        with_real = jnp.concatenate([resid_real, resid_imag], 0)
        with_imag = jnp.concatenate([resid_imag, -resid_real], 0)
        for column in range(0, width, BLOCK):
            block = slice(column, column + BLOCK)
            out_ref[local, :, block] = jnp.dot(
                with_real, real_matrix[:, block], preferred_element_type=jnp.float32
            ) + jnp.dot(with_imag, imag_matrix[:, block], preferred_element_type=jnp.float32)


def in_hbm(value):
    return pltpu.with_memory_space_constraint(value, pltpu.HBM)


def in_vmem(value):
    return pltpu.with_memory_space_constraint(value, pltpu.VMEM)


def swap(value, offset, devices):
    return lax.ppermute(value, "ma", [(device, device ^ offset) for device in range(devices)])


def body(vis, transfer, band_start, comp_index, comp_amp):
    devices = lax.axis_size("ma")
    samples, _, baselines = vis.shape
    m_local, _, _, width = transfer.shape
    comps = comp_index.shape[0]
    tiles = baselines // LANES
    pieces = 2 * tiles
    size = m_local * pieces
    unit = tile_of(comps)[3]
    vmem, smem, hbm = (pl.BlockSpec(memory_space=space) for space in (pltpu.VMEM, pltpu.SMEM, pltpu.HBM))
    params = pltpu.CompilerParams(vmem_limit_bytes=VMEM_LIMIT)
    lines = vis.reshape(samples, 2, tiles, LANES).transpose(0, 2, 1, 3).reshape(samples * pieces, LANES)
    offsets = offsets_of(devices)
    index, amp = comp_index.reshape(1, comps), comp_amp.T
    index_other = swap(comp_index, offsets[0], devices).reshape(1, comps)
    amp_other = swap(comp_amp, offsets[0], devices).T
    table = pl.pallas_call(
        functools.partial(table_kernel, samples * devices, m_local),
        out_shape=pltpu.VMEM((4 * m_local * devices, samples), jnp.bfloat16),
        in_specs=[smem],
        out_specs=vmem,
        compiler_params=params,
        cost_estimate=pl.CostEstimate(flops=LEAD, transcendentals=0, bytes_accessed=0),
        name="table",
    )(band_start)
    part = pltpu.VMEM((devices // 2 * size, LANES), jnp.float32)
    send, spectra = pl.pallas_call(
        functools.partial(transform_kernel, samples * devices, m_local),
        out_shape=(part, part),
        in_specs=[vmem, vmem],
        out_specs=(vmem, vmem),
        compiler_params=params,
        name="transform",
    )(in_vmem(table), in_vmem(lines))
    components = pl.pallas_call(
        pack_kernel,
        out_shape=pltpu.VMEM((unit, LANES), jnp.float32),
        in_specs=[vmem, hbm, hbm, vmem, vmem],
        out_specs=vmem,
        scratch_shapes=[
            pltpu.VMEM((1, comps), jnp.int32),
            pltpu.VMEM((2, comps), jnp.int32),
            pltpu.SemaphoreType.DMA((2,)),
        ],
        compiler_params=params,
        name="pack",
    )(in_vmem(spectra), in_hbm(index), in_hbm(amp), in_vmem(index_other), in_vmem(amp_other))
    got = swap(send, offsets[0], devices)
    for step, offset in enumerate(offsets[1:], 1):
        first = got.shape[0] - spectra.shape[0]
        if step == 2:
            components = components + got[:first]
        elif step > 2:
            components = jnp.concatenate([components, got[:first]], 0)
        spectra = spectra + got[first:]
        going = spectra.shape[0] // 2
        send = jnp.concatenate([components, spectra[:going]], 0)
        if step == 1:
            matrices = pl.pallas_call(
                fetch_kernel,
                out_shape=pltpu.VMEM(transfer.shape, transfer.dtype),
                in_specs=[vmem, hbm],
                out_specs=vmem,
                scratch_shapes=[pltpu.SemaphoreType.DMA],
                compiler_params=params,
                name="fetch",
            )(in_vmem(send), in_hbm(transfer))
        got, spectra = swap(send, offset, devices), spectra[going:]
    count = pl.pallas_call(
        functools.partial(count_kernel, m_local, width, comps),
        out_shape=pltpu.VMEM((m_local, 4 * width // LANES, LANES), jnp.float32),
        in_specs=[vmem],
        out_specs=vmem,
        compiler_params=params,
        name="count",
    )(in_vmem(components))
    return pl.pallas_call(
        functools.partial(residual_kernel, m_local, pieces, comps),
        out_shape=jax.ShapeDtypeStruct((m_local, 2, width), jnp.float32),
        in_specs=[vmem, vmem, vmem, vmem],
        out_specs=vmem,
        compiler_params=params,
        name="residual",
    )(in_vmem(count), in_vmem(spectra), in_vmem(got), in_vmem(matrices))


def solution(mesh):
    in_specs = (
        P(("grp", "ma"), None, None),
        P(("grp", "ma"), None, None, None),
        P("grp"),
        P(("grp", "ma")),
        P(("grp", "ma"), None),
    )
    out_specs = P(("grp", "ma"), None, None)
    return jax.shard_map(body, mesh=mesh, in_specs=in_specs, out_specs=out_specs, check_vma=False)
```

```python
import functools
import math

import jax
import jax.numpy as jnp
from jax import lax
from jax.experimental import pallas as pl
from jax.experimental.pallas import tpu as pltpu
from jax.sharding import PartitionSpec as P

LANE_BITS = 7
LANES = 1 << LANE_BITS
SPLIT_BITS = 6
SPLIT = 1 << SPLIT_BITS
NT = (((1,), (1,)), ((), ()))
BLOCK = 256
UNIT = 1.0 / 1024.0
VMEM_LIMIT = 32 * 2**20
LEAD = 400000000


def padded(count, unit):
    return -(-count // unit) * unit


def cos_sin(phase, ticks):
    quarter = ticks // 4
    quadrant = (phase + quarter // 2) >> (quarter.bit_length() - 1)
    theta = (phase - quadrant * quarter).astype(jnp.float32) * (2.0 * math.pi / ticks)
    sq = theta * theta
    sine = theta * (1.0 + sq * (-1.0 / 6 + sq * (1.0 / 120 + sq * (-1.0 / 5040 + sq * (1.0 / 362880)))))
    cosine = 1.0 + sq * (-0.5 + sq * (1.0 / 24 + sq * (-1.0 / 720 + sq * (1.0 / 40320 - sq * (1.0 / 3628800)))))
    odd = (quadrant & 1) == 1
    cos_value = jnp.where(odd, sine, cosine)
    sin_value = jnp.where(odd, cosine, sine)
    cos_value = jnp.where(((quadrant + 1) & 2) == 2, -cos_value, cos_value)
    sin_value = jnp.where((quadrant & 2) == 2, -sin_value, sin_value)
    return cos_value, sin_value


def halves(value):
    high = value.astype(jnp.bfloat16)
    low = (value - high.astype(jnp.float32)).astype(jnp.bfloat16)
    return high, low


def offsets_of(devices):
    return [1] + [step | 1 for step in (1 << bit for bit in range(1, devices.bit_length() - 1))]


def tile_of(comps):
    lanes = LANES // 2 if comps <= LANES // 2 else LANES
    lines = -(-comps // lanes)
    parts = 4 * lanes // LANES
    return lanes, lines, parts, padded(3 * lines * parts, 8)


def table_kernel(ticks, m_local, band_ref, table_ref):
    rank = lax.axis_index("ma")
    modes, samples = table_ref.shape[0] // 4, table_ref.shape[1]
    devices = modes // m_local
    row = lax.broadcasted_iota(jnp.int32, (modes, samples), 0)
    position = row % devices
    receiver = jnp.broadcast_to(rank, (modes, samples))
    for step, offset in enumerate(offsets_of(devices)):
        receiver ^= jnp.where((position & (devices >> (step + 1))) == 0, offset, 0)
    order = band_ref[0] + receiver * m_local + row // devices
    moment = rank * samples + lax.broadcasted_iota(jnp.int32, (modes, samples), 1)
    values = [halves(value) for value in cos_sin((order * moment) & (ticks - 1), ticks)]
    for part in range(4):
        table_ref[part * modes : (part + 1) * modes] = values[part % 2][part // 2]


def pack_kernel(after_ref, index_hbm, amp_hbm, index_other_ref, amp_other_ref, tile_ref, index_ref, amp_ref, sems):
    copies = [
        pltpu.make_async_copy(index_hbm, index_ref, sems.at[0]),
        pltpu.make_async_copy(amp_hbm, amp_ref, sems.at[1]),
    ]
    for copy in copies:
        copy.start()
    comps = index_ref.shape[1]
    lanes, lines, _, _ = tile_of(comps)
    shared = LANES // lanes
    tile_ref[...] = jnp.zeros(tile_ref.shape, jnp.float32)
    for copy in copies:
        copy.wait()
    lane = lax.broadcasted_iota(jnp.int32, (1, LANES), 1) // lanes
    own = lax.axis_index("ma")
    other = own ^ 1
    for which in range(3):
        for line in range(lines):
            rows = []
            for index, amp in ((index_ref, amp_ref), (index_other_ref, amp_other_ref)):
                source = index[...] if which == 0 else amp[which - 1 : which, :]
                value = source[:, line * lanes : (line + 1) * lanes].astype(jnp.float32)
                if value.shape[1] < lanes:
                    value = jnp.concatenate([value, jnp.zeros((1, lanes - value.shape[1]), jnp.float32)], 1)
                rows.append(jnp.concatenate([value] * shared, 1))
            place = which * lines + line
            if shared == 2:
                value = jnp.where(lane == own % 2, rows[0], rows[1])
                tile_ref[pl.ds(3 * lines * (own % 4 // 2) + place, 1), :] = value
            else:
                tile_ref[pl.ds(3 * lines * (own % 4) + place, 1), :] = rows[0]
                tile_ref[pl.ds(3 * lines * (other % 4) + place, 1), :] = rows[1]


def transform_kernel(ticks, m_local, table_ref, vis_ref, send_ref, keep_ref):
    modes, samples = table_ref.shape[0] // 4, table_ref.shape[1]
    devices = modes // m_local
    pieces = vis_ref.shape[0] // samples
    tiles = pieces // 2
    half, size = devices // 2, m_local * pieces
    scale = 1.0 / math.sqrt(ticks)
    for tile in range(tiles):
        parts = [vis_ref[pl.ds(tile * 2 + part, samples, stride=pieces), :] for part in range(2)]
        high, low = halves(jnp.concatenate(parts, 1))
        product = jnp.dot(table_ref[...], high, preferred_element_type=jnp.float32)
        product += jnp.dot(table_ref[...], low, preferred_element_type=jnp.float32)
        product = product[: 2 * modes] + product[2 * modes :]
        from_cos, from_sin = product[:modes], product[modes:]
        real_part = (from_cos[:, :LANES] + from_sin[:, LANES:]) * scale
        imag_part = (from_cos[:, LANES:] - from_sin[:, :LANES]) * scale
        for local in range(m_local):
            for part, value in enumerate((real_part, imag_part)):
                start = local * pieces + part * tiles + tile
                at = local * devices
                send_ref[pl.ds(start, half, stride=size), :] = value[at : at + half]
                keep_ref[pl.ds(start, half, stride=size), :] = value[at + half : at + devices]


def fetch_kernel(after_ref, transfer_hbm, transfer_ref, sem):
    copy = pltpu.make_async_copy(transfer_hbm, transfer_ref, sem)
    copy.start()
    copy.wait()


def counts_of(components, comps, base, groups):
    _, lines, parts, rows = tile_of(comps)
    numbers = components.astype(jnp.int32)
    group, place = (numbers - base) >> LANE_BITS, (numbers - base) & (LANES - 1)
    high, low = (numbers >> SPLIT_BITS).astype(jnp.float32), (numbers & (SPLIT - 1)).astype(jnp.float32)
    slot = lax.broadcasted_iota(jnp.int32, (groups, LANES), 0)
    lane = lax.broadcasted_iota(jnp.int32, (LANES, LANES), 0)
    selected, places = [], []
    for tile in range(components.shape[0] // rows):
        for part in range(parts):
            for line in range(lines):
                at = tile * rows + 3 * lines * part + line
                here = group[at : at + 1] == slot
                column = []
                for field in (at + lines, at + 2 * lines):
                    column += [jnp.where(here, value[field : field + 1], 0.0) for value in (high, low)]
                selected.append(jnp.concatenate(column, 0).astype(jnp.bfloat16))
                places.append(jnp.where(place[at : at + 1] == lane, 1.0, 0.0).astype(jnp.bfloat16))
    return lax.dot_general(
        jnp.concatenate(selected, 1), jnp.concatenate(places, 1), NT, preferred_element_type=jnp.float32
    )


def count_kernel(m_local, width, comps, held_ref, count_ref):
    groups = width // LANES
    for local in range(m_local):
        base = (lax.axis_index("ma") * m_local + local) * width
        count_ref[local] = counts_of(held_ref[...], comps, base, groups)


def residual_kernel(m_local, pieces, comps, count_ref, held_ref, got_ref, transfer_ref, turned_ref, out_ref):
    width = transfer_ref.shape[3]
    tiles = pieces // 2
    groups = width // LANES
    size = m_local * pieces
    first = got_ref.shape[0] - size
    spectra = held_ref[...] + got_ref[first:]
    for local in range(m_local):
        base = (lax.axis_index("ma") * m_local + local) * width
        counted = (count_ref[local] + counts_of(got_ref[:first], comps, base, groups)).astype(jnp.int32)
        model = []
        for part in range(2):
            high = counted[2 * part * groups : (2 * part + 1) * groups]
            low = counted[(2 * part + 1) * groups : (2 * part + 2) * groups]
            alm = ((high << SPLIT_BITS) + low).astype(jnp.float32) * UNIT
            model.append(jnp.concatenate([alm[g : g + 1] for g in range(groups)], 1))
        model_alm = jnp.concatenate(model, 0).astype(jnp.bfloat16)

        real_matrix, imag_matrix = transfer_ref[local, 0], transfer_ref[local, 1]
        predicted = jnp.dot(model_alm, turned_ref[local], preferred_element_type=jnp.float32)
        by_real, by_imag = predicted[:, : tiles * LANES], predicted[:, tiles * LANES :]
        pred_real = by_real[0:1] - by_imag[1:2]
        pred_imag = by_real[1:2] + by_imag[0:1]
        start = local * pieces
        spectrum = [
            jnp.concatenate([spectra[start + part * tiles + t : start + part * tiles + t + 1] for t in range(tiles)], 1)
            for part in range(2)
        ]
        resid_real = (spectrum[0] - pred_real).astype(jnp.bfloat16)
        resid_imag = (spectrum[1] - pred_imag).astype(jnp.bfloat16)
        with_real = jnp.concatenate([resid_real, resid_imag], 0)
        with_imag = jnp.concatenate([resid_imag, -resid_real], 0)
        for column in range(0, width, BLOCK):
            block = slice(column, column + BLOCK)
            out_ref[local, :, block] = jnp.dot(
                with_real, real_matrix[:, block], preferred_element_type=jnp.float32
            ) + jnp.dot(with_imag, imag_matrix[:, block], preferred_element_type=jnp.float32)


def turn_kernel(after_ref, transfer_ref, turned_ref):
    m_local, _, baselines, _ = transfer_ref.shape
    for local in range(m_local):
        for part in range(2):
            turned_ref[local, :, part * baselines : (part + 1) * baselines] = transfer_ref[local, part].T


def in_hbm(value):
    return pltpu.with_memory_space_constraint(value, pltpu.HBM)


def in_vmem(value):
    return pltpu.with_memory_space_constraint(value, pltpu.VMEM)


def swap(value, offset, devices):
    return lax.ppermute(value, "ma", [(device, device ^ offset) for device in range(devices)])


def body(vis, transfer, band_start, comp_index, comp_amp):
    devices = lax.axis_size("ma")
    samples, _, baselines = vis.shape
    m_local, _, _, width = transfer.shape
    comps = comp_index.shape[0]
    tiles = baselines // LANES
    pieces = 2 * tiles
    size = m_local * pieces
    unit = tile_of(comps)[3]
    vmem, smem, hbm = (pl.BlockSpec(memory_space=space) for space in (pltpu.VMEM, pltpu.SMEM, pltpu.HBM))
    params = pltpu.CompilerParams(vmem_limit_bytes=VMEM_LIMIT)
    lines = vis.reshape(samples, 2, tiles, LANES).transpose(0, 2, 1, 3).reshape(samples * pieces, LANES)
    offsets = offsets_of(devices)
    index, amp = comp_index.reshape(1, comps), comp_amp.T
    index_other = swap(comp_index, offsets[0], devices).reshape(1, comps)
    amp_other = swap(comp_amp, offsets[0], devices).T
    table = pl.pallas_call(
        functools.partial(table_kernel, samples * devices, m_local),
        out_shape=pltpu.VMEM((4 * m_local * devices, samples), jnp.bfloat16),
        in_specs=[smem],
        out_specs=vmem,
        compiler_params=params,
        cost_estimate=pl.CostEstimate(flops=LEAD, transcendentals=0, bytes_accessed=0),
        name="table",
    )(band_start)
    part = pltpu.VMEM((devices // 2 * size, LANES), jnp.float32)
    send, spectra = pl.pallas_call(
        functools.partial(transform_kernel, samples * devices, m_local),
        out_shape=(part, part),
        in_specs=[vmem, vmem],
        out_specs=(vmem, vmem),
        compiler_params=params,
        name="transform",
    )(in_vmem(table), in_vmem(lines))
    components = pl.pallas_call(
        pack_kernel,
        out_shape=pltpu.VMEM((unit, LANES), jnp.float32),
        in_specs=[vmem, hbm, hbm, vmem, vmem],
        out_specs=vmem,
        scratch_shapes=[
            pltpu.VMEM((1, comps), jnp.int32),
            pltpu.VMEM((2, comps), jnp.int32),
            pltpu.SemaphoreType.DMA((2,)),
        ],
        compiler_params=params,
        name="pack",
    )(in_vmem(spectra), in_hbm(index), in_hbm(amp), in_vmem(index_other), in_vmem(amp_other))
    got = swap(send, offsets[0], devices)
    for step, offset in enumerate(offsets[1:], 1):
        first = got.shape[0] - spectra.shape[0]
        if step == 2:
            components = components + got[:first]
        elif step > 2:
            components = jnp.concatenate([components, got[:first]], 0)
        spectra = spectra + got[first:]
        going = spectra.shape[0] // 2
        send = jnp.concatenate([components, spectra[:going]], 0)
        if step == 1:
            matrices = pl.pallas_call(
                fetch_kernel,
                out_shape=pltpu.VMEM(transfer.shape, transfer.dtype),
                in_specs=[vmem, hbm],
                out_specs=vmem,
                scratch_shapes=[pltpu.SemaphoreType.DMA],
                compiler_params=params,
                name="fetch",
            )(in_vmem(send), in_hbm(transfer))
        got, spectra = swap(send, offset, devices), spectra[going:]
    count = pl.pallas_call(
        functools.partial(count_kernel, m_local, width, comps),
        out_shape=pltpu.VMEM((m_local, 4 * width // LANES, LANES), jnp.float32),
        in_specs=[vmem],
        out_specs=vmem,
        compiler_params=params,
        name="count",
    )(in_vmem(components))
    turned = pl.pallas_call(
        turn_kernel,
        out_shape=pltpu.VMEM((m_local, width, 2 * baselines), transfer.dtype),
        in_specs=[vmem, vmem],
        out_specs=vmem,
        compiler_params=params,
        name="turn",
    )(in_vmem(components), in_vmem(matrices))
    return pl.pallas_call(
        functools.partial(residual_kernel, m_local, pieces, comps),
        out_shape=jax.ShapeDtypeStruct((m_local, 2, width), jnp.float32),
        in_specs=[vmem] * 5,
        out_specs=vmem,
        compiler_params=params,
        name="residual",
    )(in_vmem(count), in_vmem(spectra), in_vmem(got), in_vmem(matrices), in_vmem(turned))


def solution(mesh):
    in_specs = (
        P(("grp", "ma"), None, None),
        P(("grp", "ma"), None, None, None),
        P("grp"),
        P(("grp", "ma")),
        P(("grp", "ma"), None),
    )
    out_specs = P(("grp", "ma"), None, None)
    return jax.shard_map(body, mesh=mesh, in_specs=in_specs, out_specs=out_specs, check_vma=False)
```

```python
import functools
import math

import jax
import jax.numpy as jnp
from jax import lax
from jax.experimental import pallas as pl
from jax.experimental.pallas import tpu as pltpu
from jax.sharding import PartitionSpec as P

LANE_BITS = 7
LANES = 1 << LANE_BITS
SPLIT_BITS = 6
SPLIT = 1 << SPLIT_BITS
NT = (((1,), (1,)), ((), ()))
BLOCK = 256
UNIT = 1.0 / 1024.0
VMEM_LIMIT = 32 * 2**20
LEAD = 400000000


def padded(count, unit):
    return -(-count // unit) * unit


def cos_sin(phase, ticks):
    quarter = ticks // 4
    quadrant = (phase + quarter // 2) >> (quarter.bit_length() - 1)
    theta = (phase - quadrant * quarter).astype(jnp.float32) * (2.0 * math.pi / ticks)
    sq = theta * theta
    sine = theta * (1.0 + sq * (-1.0 / 6 + sq * (1.0 / 120 + sq * (-1.0 / 5040 + sq * (1.0 / 362880)))))
    cosine = 1.0 + sq * (-0.5 + sq * (1.0 / 24 + sq * (-1.0 / 720 + sq * (1.0 / 40320 - sq * (1.0 / 3628800)))))
    odd = (quadrant & 1) == 1
    cos_value = jnp.where(odd, sine, cosine)
    sin_value = jnp.where(odd, cosine, sine)
    cos_value = jnp.where(((quadrant + 1) & 2) == 2, -cos_value, cos_value)
    sin_value = jnp.where((quadrant & 2) == 2, -sin_value, sin_value)
    return cos_value, sin_value


def halves(value):
    high = value.astype(jnp.bfloat16)
    low = (value - high.astype(jnp.float32)).astype(jnp.bfloat16)
    return high, low


def offsets_of(devices):
    return [1] + [step | 1 for step in (1 << bit for bit in range(1, devices.bit_length() - 1))]


def tile_of(comps):
    lanes = LANES // 2 if comps <= LANES // 2 else LANES
    lines = -(-comps // lanes)
    parts = 4 * lanes // LANES
    return lanes, lines, parts, padded(3 * lines * parts, 8)


def table_kernel(ticks, m_local, band_ref, table_ref):
    rank = lax.axis_index("ma")
    modes, samples = table_ref.shape[0] // 4, table_ref.shape[1]
    devices = modes // m_local
    row = lax.broadcasted_iota(jnp.int32, (modes, samples), 0)
    position = row % devices
    receiver = jnp.broadcast_to(rank, (modes, samples))
    for step, offset in enumerate(offsets_of(devices)):
        receiver ^= jnp.where((position & (devices >> (step + 1))) == 0, offset, 0)
    order = band_ref[0] + receiver * m_local + row // devices
    moment = rank * samples + lax.broadcasted_iota(jnp.int32, (modes, samples), 1)
    values = [halves(value) for value in cos_sin((order * moment) & (ticks - 1), ticks)]
    for part in range(4):
        table_ref[part * modes : (part + 1) * modes] = values[part % 2][part // 2]


def pack_kernel(after_ref, index_hbm, amp_hbm, index_other_ref, amp_other_ref, tile_ref, index_ref, amp_ref, sems):
    copies = [
        pltpu.make_async_copy(index_hbm, index_ref, sems.at[0]),
        pltpu.make_async_copy(amp_hbm, amp_ref, sems.at[1]),
    ]
    for copy in copies:
        copy.start()
    comps = index_ref.shape[1]
    lanes, lines, _, _ = tile_of(comps)
    shared = LANES // lanes
    tile_ref[...] = jnp.zeros(tile_ref.shape, jnp.float32)
    for copy in copies:
        copy.wait()
    lane = lax.broadcasted_iota(jnp.int32, (1, LANES), 1) // lanes
    own = lax.axis_index("ma")
    other = own ^ 1
    for which in range(3):
        for line in range(lines):
            rows = []
            for index, amp in ((index_ref, amp_ref), (index_other_ref, amp_other_ref)):
                source = index[...] if which == 0 else amp[which - 1 : which, :]
                value = source[:, line * lanes : (line + 1) * lanes].astype(jnp.float32)
                if value.shape[1] < lanes:
                    value = jnp.concatenate([value, jnp.zeros((1, lanes - value.shape[1]), jnp.float32)], 1)
                rows.append(jnp.concatenate([value] * shared, 1))
            place = which * lines + line
            if shared == 2:
                value = jnp.where(lane == own % 2, rows[0], rows[1])
                tile_ref[pl.ds(3 * lines * (own % 4 // 2) + place, 1), :] = value
            else:
                tile_ref[pl.ds(3 * lines * (own % 4) + place, 1), :] = rows[0]
                tile_ref[pl.ds(3 * lines * (other % 4) + place, 1), :] = rows[1]


def transform_kernel(ticks, m_local, table_ref, vis_ref, send_ref, keep_ref):
    modes, samples = table_ref.shape[0] // 4, table_ref.shape[1]
    devices = modes // m_local
    pieces = vis_ref.shape[0] // samples
    tiles = pieces // 2
    half, size = devices // 2, m_local * pieces
    scale = 1.0 / math.sqrt(ticks)
    steps = 4 if samples % 64 == 0 else 1
    depth = samples // steps
    for tile in range(tiles):
        product, smaller = 0.0, 0.0
        for step in range(steps):
            first = step * depth
            parts = [vis_ref[pl.ds(first * pieces + tile * 2 + part, depth, stride=pieces), :] for part in range(2)]
            high, low = halves(jnp.concatenate(parts, 1))
            columns = slice(first, first + depth)
            product += jnp.dot(table_ref[:, columns], high, preferred_element_type=jnp.float32)
            smaller += jnp.dot(table_ref[: 2 * modes, columns], low, preferred_element_type=jnp.float32)
        product = product[: 2 * modes] + (product[2 * modes :] + smaller)
        from_cos, from_sin = product[:modes], product[modes:]
        real_part = (from_cos[:, :LANES] + from_sin[:, LANES:]) * scale
        imag_part = (from_cos[:, LANES:] - from_sin[:, :LANES]) * scale
        for local in range(m_local):
            for part, value in enumerate((real_part, imag_part)):
                start = local * pieces + part * tiles + tile
                at = local * devices
                send_ref[pl.ds(start, half, stride=size), :] = value[at : at + half]
                keep_ref[pl.ds(start, half, stride=size), :] = value[at + half : at + devices]


def fetch_kernel(after_ref, transfer_hbm, transfer_ref, sem):
    copy = pltpu.make_async_copy(transfer_hbm, transfer_ref, sem)
    copy.start()
    copy.wait()


def counts_of(components, comps, base, groups):
    _, lines, parts, rows = tile_of(comps)
    numbers = components.astype(jnp.int32)
    group, place = (numbers - base) >> LANE_BITS, (numbers - base) & (LANES - 1)
    high, low = (numbers >> SPLIT_BITS).astype(jnp.float32), (numbers & (SPLIT - 1)).astype(jnp.float32)
    slot = lax.broadcasted_iota(jnp.int32, (groups, LANES), 0)
    lane = lax.broadcasted_iota(jnp.int32, (LANES, LANES), 0)
    selected, places = [], []
    for tile in range(components.shape[0] // rows):
        for part in range(parts):
            for line in range(lines):
                at = tile * rows + 3 * lines * part + line
                here = group[at : at + 1] == slot
                column = []
                for field in (at + lines, at + 2 * lines):
                    column += [jnp.where(here, value[field : field + 1], 0.0) for value in (high, low)]
                selected.append(jnp.concatenate(column, 0).astype(jnp.bfloat16))
                places.append(jnp.where(place[at : at + 1] == lane, 1.0, 0.0).astype(jnp.bfloat16))
    return lax.dot_general(
        jnp.concatenate(selected, 1), jnp.concatenate(places, 1), NT, preferred_element_type=jnp.float32
    )


def count_kernel(m_local, width, comps, held_ref, count_ref):
    groups = width // LANES
    for local in range(m_local):
        base = (lax.axis_index("ma") * m_local + local) * width
        count_ref[local] = counts_of(held_ref[...], comps, base, groups)


def residual_kernel(m_local, pieces, comps, count_ref, held_ref, got_ref, transfer_ref, turned_ref, out_ref):
    width = transfer_ref.shape[3]
    tiles = pieces // 2
    groups = width // LANES
    size = m_local * pieces
    first = got_ref.shape[0] - size
    spectra = held_ref[...] + got_ref[first:]
    for local in range(m_local):
        base = (lax.axis_index("ma") * m_local + local) * width
        counted = (count_ref[local] + counts_of(got_ref[:first], comps, base, groups)).astype(jnp.int32)
        model = []
        for part in range(2):
            high = counted[2 * part * groups : (2 * part + 1) * groups]
            low = counted[(2 * part + 1) * groups : (2 * part + 2) * groups]
            alm = ((high << SPLIT_BITS) + low).astype(jnp.float32) * UNIT
            model.append(jnp.concatenate([alm[g : g + 1] for g in range(groups)], 1))
        model_alm = jnp.concatenate(model, 0).astype(jnp.bfloat16)

        real_matrix, imag_matrix = transfer_ref[local, 0], transfer_ref[local, 1]
        predicted = jnp.dot(model_alm, turned_ref[local], preferred_element_type=jnp.float32)
        by_real, by_imag = predicted[:, : tiles * LANES], predicted[:, tiles * LANES :]
        pred_real = by_real[0:1] - by_imag[1:2]
        pred_imag = by_real[1:2] + by_imag[0:1]
        start = local * pieces
        spectrum = [
            jnp.concatenate([spectra[start + part * tiles + t : start + part * tiles + t + 1] for t in range(tiles)], 1)
            for part in range(2)
        ]
        resid_real = (spectrum[0] - pred_real).astype(jnp.bfloat16)
        resid_imag = (spectrum[1] - pred_imag).astype(jnp.bfloat16)
        with_real = jnp.concatenate([resid_real, resid_imag], 0)
        with_imag = jnp.concatenate([resid_imag, -resid_real], 0)
        for column in range(0, width, BLOCK):
            block = slice(column, column + BLOCK)
            out_ref[local, :, block] = jnp.dot(
                with_real, real_matrix[:, block], preferred_element_type=jnp.float32
            ) + jnp.dot(with_imag, imag_matrix[:, block], preferred_element_type=jnp.float32)


def turn_kernel(after_ref, transfer_ref, turned_ref):
    m_local, _, baselines, _ = transfer_ref.shape
    for local in range(m_local):
        for part in range(2):
            turned_ref[local, :, part * baselines : (part + 1) * baselines] = transfer_ref[local, part].T


def in_hbm(value):
    return pltpu.with_memory_space_constraint(value, pltpu.HBM)


def in_vmem(value):
    return pltpu.with_memory_space_constraint(value, pltpu.VMEM)


def swap(value, offset, devices):
    return lax.ppermute(value, "ma", [(device, device ^ offset) for device in range(devices)])


def body(vis, transfer, band_start, comp_index, comp_amp):
    devices = lax.axis_size("ma")
    samples, _, baselines = vis.shape
    m_local, _, _, width = transfer.shape
    comps = comp_index.shape[0]
    tiles = baselines // LANES
    pieces = 2 * tiles
    size = m_local * pieces
    unit = tile_of(comps)[3]
    vmem, smem, hbm = (pl.BlockSpec(memory_space=space) for space in (pltpu.VMEM, pltpu.SMEM, pltpu.HBM))
    params = pltpu.CompilerParams(vmem_limit_bytes=VMEM_LIMIT)
    lines = vis.reshape(samples, 2, tiles, LANES).transpose(0, 2, 1, 3).reshape(samples * pieces, LANES)
    offsets = offsets_of(devices)
    index, amp = comp_index.reshape(1, comps), comp_amp.T
    index_other = swap(comp_index, offsets[0], devices).reshape(1, comps)
    amp_other = swap(comp_amp, offsets[0], devices).T
    table = pl.pallas_call(
        functools.partial(table_kernel, samples * devices, m_local),
        out_shape=pltpu.VMEM((4 * m_local * devices, samples), jnp.bfloat16),
        in_specs=[smem],
        out_specs=vmem,
        compiler_params=params,
        cost_estimate=pl.CostEstimate(flops=LEAD, transcendentals=0, bytes_accessed=0),
        name="table",
    )(band_start)
    part = pltpu.VMEM((devices // 2 * size, LANES), jnp.float32)
    send, spectra = pl.pallas_call(
        functools.partial(transform_kernel, samples * devices, m_local),
        out_shape=(part, part),
        in_specs=[vmem, vmem],
        out_specs=(vmem, vmem),
        compiler_params=params,
        name="transform",
    )(in_vmem(table), in_vmem(lines))
    components = pl.pallas_call(
        pack_kernel,
        out_shape=pltpu.VMEM((unit, LANES), jnp.float32),
        in_specs=[vmem, hbm, hbm, vmem, vmem],
        out_specs=vmem,
        scratch_shapes=[
            pltpu.VMEM((1, comps), jnp.int32),
            pltpu.VMEM((2, comps), jnp.int32),
            pltpu.SemaphoreType.DMA((2,)),
        ],
        compiler_params=params,
        name="pack",
    )(in_vmem(spectra), in_hbm(index), in_hbm(amp), in_vmem(index_other), in_vmem(amp_other))
    got = swap(send, offsets[0], devices)
    for step, offset in enumerate(offsets[1:], 1):
        first = got.shape[0] - spectra.shape[0]
        if step == 2:
            components = components + got[:first]
        elif step > 2:
            components = jnp.concatenate([components, got[:first]], 0)
        spectra = spectra + got[first:]
        going = spectra.shape[0] // 2
        send = jnp.concatenate([components, spectra[:going]], 0)
        if step == 1:
            matrices = pl.pallas_call(
                fetch_kernel,
                out_shape=pltpu.VMEM(transfer.shape, transfer.dtype),
                in_specs=[vmem, hbm],
                out_specs=vmem,
                scratch_shapes=[pltpu.SemaphoreType.DMA],
                compiler_params=params,
                name="fetch",
            )(in_vmem(send), in_hbm(transfer))
        got, spectra = swap(send, offset, devices), spectra[going:]
    count = pl.pallas_call(
        functools.partial(count_kernel, m_local, width, comps),
        out_shape=pltpu.VMEM((m_local, 4 * width // LANES, LANES), jnp.float32),
        in_specs=[vmem],
        out_specs=vmem,
        compiler_params=params,
        name="count",
    )(in_vmem(components))
    turned = pl.pallas_call(
        turn_kernel,
        out_shape=pltpu.VMEM((m_local, width, 2 * baselines), transfer.dtype),
        in_specs=[vmem, vmem],
        out_specs=vmem,
        compiler_params=params,
        name="turn",
    )(in_vmem(components), in_vmem(matrices))
    return pl.pallas_call(
        functools.partial(residual_kernel, m_local, pieces, comps),
        out_shape=jax.ShapeDtypeStruct((m_local, 2, width), jnp.float32),
        in_specs=[vmem] * 5,
        out_specs=vmem,
        compiler_params=params,
        name="residual",
    )(in_vmem(count), in_vmem(spectra), in_vmem(got), in_vmem(matrices), in_vmem(turned))


def solution(mesh):
    in_specs = (
        P(("grp", "ma"), None, None),
        P(("grp", "ma"), None, None, None),
        P("grp"),
        P(("grp", "ma")),
        P(("grp", "ma"), None),
    )
    out_specs = P(("grp", "ma"), None, None)
    return jax.shard_map(body, mesh=mesh, in_specs=in_specs, out_specs=out_specs, check_vma=False)
```

```python
import functools
import math

import jax
import jax.numpy as jnp
from jax import lax
from jax.experimental import pallas as pl
from jax.experimental.pallas import tpu as pltpu
from jax.sharding import PartitionSpec as P

LANE_BITS = 7
LANES = 1 << LANE_BITS
SPLIT_BITS = 6
SPLIT = 1 << SPLIT_BITS
NT = (((1,), (1,)), ((), ()))
BLOCK = 256
UNIT = 1.0 / 1024.0
VMEM_LIMIT = 32 * 2**20
LEAD = 400000000


def padded(count, unit):
    return -(-count // unit) * unit


def cos_sin(phase, ticks):
    quarter = ticks // 4
    quadrant = (phase + quarter // 2) >> (quarter.bit_length() - 1)
    theta = (phase - quadrant * quarter).astype(jnp.float32) * (2.0 * math.pi / ticks)
    sq = theta * theta
    sine = theta * (1.0 + sq * (-1.0 / 6 + sq * (1.0 / 120 + sq * (-1.0 / 5040 + sq * (1.0 / 362880)))))
    cosine = 1.0 + sq * (-0.5 + sq * (1.0 / 24 + sq * (-1.0 / 720 + sq * (1.0 / 40320 - sq * (1.0 / 3628800)))))
    odd = (quadrant & 1) == 1
    cos_value = jnp.where(odd, sine, cosine)
    sin_value = jnp.where(odd, cosine, sine)
    cos_value = jnp.where(((quadrant + 1) & 2) == 2, -cos_value, cos_value)
    sin_value = jnp.where((quadrant & 2) == 2, -sin_value, sin_value)
    return cos_value, sin_value


def halves(value):
    high = value.astype(jnp.bfloat16)
    low = (value - high.astype(jnp.float32)).astype(jnp.bfloat16)
    return high, low


def offsets_of(devices):
    return [1] + [step | 1 for step in (1 << bit for bit in range(1, devices.bit_length() - 1))]


def tile_of(comps):
    lanes = LANES // 2 if comps <= LANES // 2 else LANES
    lines = -(-comps // lanes)
    parts = 4 * lanes // LANES
    return lanes, lines, parts, padded(3 * lines * parts, 8)


def table_kernel(ticks, m_local, band_ref, table_ref):
    rank = lax.axis_index("ma")
    modes, samples = table_ref.shape[0] // 4, table_ref.shape[1]
    devices = modes // m_local
    row = lax.broadcasted_iota(jnp.int32, (modes, samples), 0)
    position = row % devices
    receiver = jnp.broadcast_to(rank, (modes, samples))
    for step, offset in enumerate(offsets_of(devices)):
        receiver ^= jnp.where((position & (devices >> (step + 1))) == 0, offset, 0)
    order = band_ref[0] + receiver * m_local + row // devices
    moment = rank * samples + lax.broadcasted_iota(jnp.int32, (modes, samples), 1)
    values = [halves(value) for value in cos_sin((order * moment) & (ticks - 1), ticks)]
    for part in range(4):
        table_ref[part * modes : (part + 1) * modes] = values[part % 2][part // 2]


def pack_kernel(kept_ref, index_hbm, amp_hbm, index_other_ref, amp_other_ref, tile_ref, index_ref, amp_ref, sems):
    copies = [
        pltpu.make_async_copy(index_hbm, index_ref, sems.at[0]),
        pltpu.make_async_copy(amp_hbm, amp_ref, sems.at[1]),
    ]
    for copy in copies:
        copy.start()
    comps = index_ref.shape[1]
    lanes, lines, _, _ = tile_of(comps)
    shared = LANES // lanes
    unit = tile_of(comps)[3]
    tile_ref[:unit] = jnp.zeros((unit, LANES), jnp.float32)
    tile_ref[unit:] = kept_ref[...]
    for copy in copies:
        copy.wait()
    lane = lax.broadcasted_iota(jnp.int32, (1, LANES), 1) // lanes
    own = lax.axis_index("ma")
    other = own ^ 1
    for which in range(3):
        for line in range(lines):
            rows = []
            for index, amp in ((index_ref, amp_ref), (index_other_ref, amp_other_ref)):
                source = index[...] if which == 0 else amp[which - 1 : which, :]
                value = source[:, line * lanes : (line + 1) * lanes].astype(jnp.float32)
                if value.shape[1] < lanes:
                    value = jnp.concatenate([value, jnp.zeros((1, lanes - value.shape[1]), jnp.float32)], 1)
                rows.append(jnp.concatenate([value] * shared, 1))
            place = which * lines + line
            if shared == 2:
                value = jnp.where(lane == own % 2, rows[0], rows[1])
                tile_ref[pl.ds(3 * lines * (own % 4 // 2) + place, 1), :] = value
            else:
                tile_ref[pl.ds(3 * lines * (own % 4) + place, 1), :] = rows[0]
                tile_ref[pl.ds(3 * lines * (other % 4) + place, 1), :] = rows[1]


def transform_kernel(ticks, m_local, table_ref, vis_ref, send_ref, keep_ref):
    modes, samples = table_ref.shape[0] // 4, table_ref.shape[1]
    devices = modes // m_local
    pieces = vis_ref.shape[0] // samples
    tiles = pieces // 2
    half, size = devices // 2, m_local * pieces
    lead = send_ref.shape[0] - keep_ref.shape[0]
    send_ref[:lead] = jnp.zeros((lead, LANES), jnp.float32)
    scale = 1.0 / math.sqrt(ticks)
    steps = 4 if samples % 64 == 0 else 1
    depth = samples // steps
    for tile in range(tiles):
        product, smaller = 0.0, 0.0
        for step in range(steps):
            first = step * depth
            parts = [vis_ref[pl.ds(first * pieces + tile * 2 + part, depth, stride=pieces), :] for part in range(2)]
            high, low = halves(jnp.concatenate(parts, 1))
            columns = slice(first, first + depth)
            product += jnp.dot(table_ref[:, columns], high, preferred_element_type=jnp.float32)
            smaller += jnp.dot(table_ref[: 2 * modes, columns], low, preferred_element_type=jnp.float32)
        product = product[: 2 * modes] + (product[2 * modes :] + smaller)
        from_cos, from_sin = product[:modes], product[modes:]
        real_part = (from_cos[:, :LANES] + from_sin[:, LANES:]) * scale
        imag_part = (from_cos[:, LANES:] - from_sin[:, :LANES]) * scale
        for local in range(m_local):
            for part, value in enumerate((real_part, imag_part)):
                start = local * pieces + part * tiles + tile
                at = local * devices
                send_ref[pl.ds(lead + start, half, stride=size), :] = value[at : at + half]
                keep_ref[pl.ds(start, half, stride=size), :] = value[at + half : at + devices]


def fetch_kernel(after_ref, transfer_hbm, transfer_ref, sem):
    copy = pltpu.make_async_copy(transfer_hbm, transfer_ref, sem)
    copy.start()
    copy.wait()


def counts_of(components, comps, base, groups):
    _, lines, parts, rows = tile_of(comps)
    numbers = components.astype(jnp.int32)
    group, place = (numbers - base) >> LANE_BITS, (numbers - base) & (LANES - 1)
    high, low = (numbers >> SPLIT_BITS).astype(jnp.float32), (numbers & (SPLIT - 1)).astype(jnp.float32)
    slot = lax.broadcasted_iota(jnp.int32, (groups, LANES), 0)
    lane = lax.broadcasted_iota(jnp.int32, (LANES, LANES), 0)
    selected, places = [], []
    for tile in range(components.shape[0] // rows):
        for part in range(parts):
            for line in range(lines):
                at = tile * rows + 3 * lines * part + line
                here = group[at : at + 1] == slot
                column = []
                for field in (at + lines, at + 2 * lines):
                    column += [jnp.where(here, value[field : field + 1], 0.0) for value in (high, low)]
                selected.append(jnp.concatenate(column, 0).astype(jnp.bfloat16))
                places.append(jnp.where(place[at : at + 1] == lane, 1.0, 0.0).astype(jnp.bfloat16))
    return lax.dot_general(
        jnp.concatenate(selected, 1), jnp.concatenate(places, 1), NT, preferred_element_type=jnp.float32
    )


def count_kernel(m_local, width, comps, held_ref, count_ref):
    groups = width // LANES
    for local in range(m_local):
        base = (lax.axis_index("ma") * m_local + local) * width
        count_ref[local] = counts_of(held_ref[...], comps, base, groups)


def residual_kernel(m_local, pieces, comps, count_ref, held_ref, got_ref, transfer_ref, turned_ref, out_ref):
    width = transfer_ref.shape[3]
    tiles = pieces // 2
    groups = width // LANES
    size = m_local * pieces
    first = got_ref.shape[0] - size
    spectra = held_ref[...] + got_ref[first:]
    for local in range(m_local):
        base = (lax.axis_index("ma") * m_local + local) * width
        counted = (count_ref[local] + counts_of(got_ref[:first], comps, base, groups)).astype(jnp.int32)
        model = []
        for part in range(2):
            high = counted[2 * part * groups : (2 * part + 1) * groups]
            low = counted[(2 * part + 1) * groups : (2 * part + 2) * groups]
            alm = ((high << SPLIT_BITS) + low).astype(jnp.float32) * UNIT
            model.append(jnp.concatenate([alm[g : g + 1] for g in range(groups)], 1))
        model_alm = jnp.concatenate(model, 0).astype(jnp.bfloat16)

        predicted = jnp.concatenate(
            [
                jnp.dot(model_alm, turned_ref[local, :, at : at + BLOCK], preferred_element_type=jnp.float32)
                for at in range(0, 2 * tiles * LANES, BLOCK)
            ],
            1,
        )
        by_real, by_imag = predicted[:, : tiles * LANES], predicted[:, tiles * LANES :]
        pred_real = by_real[0:1] - by_imag[1:2]
        pred_imag = by_real[1:2] + by_imag[0:1]
        start = local * pieces
        spectrum = [
            jnp.concatenate([spectra[start + part * tiles + t : start + part * tiles + t + 1] for t in range(tiles)], 1)
            for part in range(2)
        ]
        resid_real = (spectrum[0] - pred_real).astype(jnp.bfloat16)
        resid_imag = (spectrum[1] - pred_imag).astype(jnp.bfloat16)
        both = jnp.concatenate(
            [jnp.concatenate([resid_real, resid_imag], 1), jnp.concatenate([resid_imag, -resid_real], 1)], 0
        )
        matrix = transfer_ref[local].reshape(2 * tiles * LANES, width)
        for column in range(0, width, BLOCK):
            block = slice(column, column + BLOCK)
            out_ref[local, :, block] = jnp.dot(both, matrix[:, block], preferred_element_type=jnp.float32)


def turn_kernel(after_ref, transfer_ref, turned_ref):
    m_local, _, baselines, _ = transfer_ref.shape
    for local in range(m_local):
        for part in range(2):
            turned_ref[local, :, part * baselines : (part + 1) * baselines] = transfer_ref[local, part].T


def in_hbm(value):
    return pltpu.with_memory_space_constraint(value, pltpu.HBM)


def in_vmem(value):
    return pltpu.with_memory_space_constraint(value, pltpu.VMEM)


def swap(value, offset, devices):
    return lax.ppermute(value, "ma", [(device, device ^ offset) for device in range(devices)])


def body(vis, transfer, band_start, comp_index, comp_amp):
    devices = lax.axis_size("ma")
    samples, _, baselines = vis.shape
    m_local, _, _, width = transfer.shape
    comps = comp_index.shape[0]
    tiles = baselines // LANES
    pieces = 2 * tiles
    size = m_local * pieces
    unit = tile_of(comps)[3]
    vmem, smem, hbm = (pl.BlockSpec(memory_space=space) for space in (pltpu.VMEM, pltpu.SMEM, pltpu.HBM))
    params = pltpu.CompilerParams(vmem_limit_bytes=VMEM_LIMIT)
    lines = vis.reshape(samples, 2, tiles, LANES).transpose(0, 2, 1, 3).reshape(samples * pieces, LANES)
    offsets = offsets_of(devices)
    index, amp = comp_index.reshape(1, comps), comp_amp.T
    index_other = swap(comp_index, offsets[0], devices).reshape(1, comps)
    amp_other = swap(comp_amp, offsets[0], devices).T
    table = pl.pallas_call(
        functools.partial(table_kernel, samples * devices, m_local),
        out_shape=pltpu.VMEM((4 * m_local * devices, samples), jnp.bfloat16),
        in_specs=[smem],
        out_specs=vmem,
        compiler_params=params,
        cost_estimate=pl.CostEstimate(flops=LEAD, transcendentals=0, bytes_accessed=0),
        name="table",
    )(band_start)
    half_rows = devices // 2 * size
    message = pltpu.VMEM((unit + half_rows, LANES), jnp.float32)
    send, kept = pl.pallas_call(
        functools.partial(transform_kernel, samples * devices, m_local),
        out_shape=(message, pltpu.VMEM((half_rows, LANES), jnp.float32)),
        in_specs=[vmem, vmem],
        out_specs=(vmem, vmem),
        compiler_params=params,
        name="transform",
    )(in_vmem(table), in_vmem(lines))
    held = pl.pallas_call(
        pack_kernel,
        out_shape=message,
        in_specs=[vmem, hbm, hbm, vmem, vmem],
        out_specs=vmem,
        scratch_shapes=[
            pltpu.VMEM((1, comps), jnp.int32),
            pltpu.VMEM((2, comps), jnp.int32),
            pltpu.SemaphoreType.DMA((2,)),
        ],
        compiler_params=params,
        name="pack",
    )(in_vmem(kept), in_hbm(index), in_hbm(amp), in_vmem(index_other), in_vmem(amp_other))
    got = swap(send, offsets[0], devices)
    first = unit
    for step, offset in enumerate(offsets[1:], 1):
        going = first + (held.shape[0] - first) // 2
        if step <= 2:
            send = held[:going] + got[:going]
            held = jnp.concatenate([held[:first] + got[:first], held[going:] + got[going:]], 0)
        else:
            parcels = [held[:first], got[:first]]
            send = jnp.concatenate(parcels + [held[first:going] + got[first:going]], 0)
            held = jnp.concatenate(parcels + [held[going:] + got[going:]], 0)
            first *= 2
        if step == 1:
            matrices = pl.pallas_call(
                fetch_kernel,
                out_shape=pltpu.VMEM(transfer.shape, transfer.dtype),
                in_specs=[vmem, hbm],
                out_specs=vmem,
                scratch_shapes=[pltpu.SemaphoreType.DMA],
                compiler_params=params,
                name="fetch",
            )(in_vmem(send), in_hbm(transfer))
        got = swap(send, offset, devices)
    components, spectra = held[:first], held[first:]
    count = pl.pallas_call(
        functools.partial(count_kernel, m_local, width, comps),
        out_shape=pltpu.VMEM((m_local, 4 * width // LANES, LANES), jnp.float32),
        in_specs=[vmem],
        out_specs=vmem,
        compiler_params=params,
        name="count",
    )(in_vmem(components))
    turned = pl.pallas_call(
        turn_kernel,
        out_shape=pltpu.VMEM((m_local, width, 2 * baselines), transfer.dtype),
        in_specs=[vmem, vmem],
        out_specs=vmem,
        compiler_params=params,
        name="turn",
    )(in_vmem(components), in_vmem(matrices))
    return pl.pallas_call(
        functools.partial(residual_kernel, m_local, pieces, comps),
        out_shape=jax.ShapeDtypeStruct((m_local, 2, width), jnp.float32),
        in_specs=[vmem] * 5,
        out_specs=vmem,
        compiler_params=params,
        name="residual",
    )(in_vmem(count), in_vmem(spectra), in_vmem(got), in_vmem(matrices), in_vmem(turned))


def solution(mesh):
    in_specs = (
        P(("grp", "ma"), None, None),
        P(("grp", "ma"), None, None, None),
        P("grp"),
        P(("grp", "ma")),
        P(("grp", "ma"), None),
    )
    out_specs = P(("grp", "ma"), None, None)
    return jax.shard_map(body, mesh=mesh, in_specs=in_specs, out_specs=out_specs, check_vma=False)
```

```python
import functools
import math

import jax
import jax.numpy as jnp
from jax import lax
from jax.experimental import pallas as pl
from jax.experimental.pallas import tpu as pltpu
from jax.sharding import PartitionSpec as P

LANE_BITS = 7
LANES = 1 << LANE_BITS
SPLIT_BITS = 6
SPLIT = 1 << SPLIT_BITS
NT = (((1,), (1,)), ((), ()))
BLOCK = 512
UNIT = 1.0 / 1024.0
VMEM_LIMIT = 32 * 2**20
LEAD = 400000000


def padded(count, unit):
    return -(-count // unit) * unit


def cos_sin(phase, ticks):
    quarter = ticks // 4
    quadrant = (phase + quarter // 2) >> (quarter.bit_length() - 1)
    theta = (phase - quadrant * quarter).astype(jnp.float32) * (2.0 * math.pi / ticks)
    sq = theta * theta
    sine = theta * (1.0 + sq * (-1.0 / 6 + sq * (1.0 / 120 + sq * (-1.0 / 5040 + sq * (1.0 / 362880)))))
    cosine = 1.0 + sq * (-0.5 + sq * (1.0 / 24 + sq * (-1.0 / 720 + sq * (1.0 / 40320 - sq * (1.0 / 3628800)))))
    odd = (quadrant & 1) == 1
    cos_value = jnp.where(odd, sine, cosine)
    sin_value = jnp.where(odd, cosine, sine)
    cos_value = jnp.where(((quadrant + 1) & 2) == 2, -cos_value, cos_value)
    sin_value = jnp.where((quadrant & 2) == 2, -sin_value, sin_value)
    return cos_value, sin_value


def halves(value):
    high = value.astype(jnp.bfloat16)
    low = (value - high.astype(jnp.float32)).astype(jnp.bfloat16)
    return high, low


def offsets_of(devices):
    return [1] + [step | 1 for step in (1 << bit for bit in range(1, devices.bit_length() - 1))]


def tile_of(comps):
    lanes = LANES // 2 if comps <= LANES // 2 else LANES
    lines = -(-comps // lanes)
    parts = 4 * lanes // LANES
    return lanes, lines, parts, padded(3 * lines * parts, 8)


def table_kernel(ticks, m_local, band_ref, table_ref):
    rank = lax.axis_index("ma")
    modes, samples = table_ref.shape[0] // 4, table_ref.shape[1]
    devices = modes // m_local
    row = lax.broadcasted_iota(jnp.int32, (modes, samples), 0)
    position = row % devices
    receiver = jnp.broadcast_to(rank, (modes, samples))
    for step, offset in enumerate(offsets_of(devices)):
        receiver ^= jnp.where((position & (devices >> (step + 1))) == 0, offset, 0)
    order = band_ref[0] + receiver * m_local + row // devices
    moment = rank * samples + lax.broadcasted_iota(jnp.int32, (modes, samples), 1)
    values = [halves(value) for value in cos_sin((order * moment) & (ticks - 1), ticks)]
    for part in range(4):
        table_ref[part * modes : (part + 1) * modes] = values[part % 2][part // 2]


def pack_kernel(kept_ref, index_hbm, amp_hbm, index_other_ref, amp_other_ref, tile_ref, index_ref, amp_ref, sems):
    copies = [
        pltpu.make_async_copy(index_hbm, index_ref, sems.at[0]),
        pltpu.make_async_copy(amp_hbm, amp_ref, sems.at[1]),
    ]
    for copy in copies:
        copy.start()
    comps = index_ref.shape[1]
    lanes, lines, _, _ = tile_of(comps)
    shared = LANES // lanes
    unit = tile_of(comps)[3]
    tile_ref[:unit] = jnp.zeros((unit, LANES), jnp.float32)
    tile_ref[unit:] = kept_ref[...]
    for copy in copies:
        copy.wait()
    lane = lax.broadcasted_iota(jnp.int32, (1, LANES), 1) // lanes
    own = lax.axis_index("ma")
    other = own ^ 1
    for which in range(3):
        for line in range(lines):
            rows = []
            for index, amp in ((index_ref, amp_ref), (index_other_ref, amp_other_ref)):
                source = index[...] if which == 0 else amp[which - 1 : which, :]
                value = source[:, line * lanes : (line + 1) * lanes].astype(jnp.float32)
                if value.shape[1] < lanes:
                    value = jnp.concatenate([value, jnp.zeros((1, lanes - value.shape[1]), jnp.float32)], 1)
                rows.append(jnp.concatenate([value] * shared, 1))
            place = which * lines + line
            if shared == 2:
                value = jnp.where(lane == own % 2, rows[0], rows[1])
                tile_ref[pl.ds(3 * lines * (own % 4 // 2) + place, 1), :] = value
            else:
                tile_ref[pl.ds(3 * lines * (own % 4) + place, 1), :] = rows[0]
                tile_ref[pl.ds(3 * lines * (other % 4) + place, 1), :] = rows[1]


def transform_kernel(ticks, m_local, table_ref, vis_ref, send_ref, keep_ref):
    modes, samples = table_ref.shape[0] // 4, table_ref.shape[1]
    devices = modes // m_local
    pieces = vis_ref.shape[0] // samples
    tiles = pieces // 2
    half, size = devices // 2, m_local * pieces
    lead = send_ref.shape[0] - keep_ref.shape[0]
    send_ref[:lead] = jnp.zeros((lead, LANES), jnp.float32)
    scale = 1.0 / math.sqrt(ticks)
    steps = 4 if samples % 64 == 0 else 1
    depth = samples // steps
    for tile in range(tiles):
        product, smaller = 0.0, 0.0
        for step in range(steps):
            first = step * depth
            parts = [vis_ref[pl.ds(first * pieces + tile * 2 + part, depth, stride=pieces), :] for part in range(2)]
            high, low = halves(jnp.concatenate(parts, 1))
            columns = slice(first, first + depth)
            product += jnp.dot(table_ref[:, columns], high, preferred_element_type=jnp.float32)
            smaller += jnp.dot(table_ref[: 2 * modes, columns], low, preferred_element_type=jnp.float32)
        product = product[: 2 * modes] + (product[2 * modes :] + smaller)
        from_cos, from_sin = product[:modes], product[modes:]
        real_part = (from_cos[:, :LANES] + from_sin[:, LANES:]) * scale
        imag_part = (from_cos[:, LANES:] - from_sin[:, :LANES]) * scale
        for local in range(m_local):
            for part, value in enumerate((real_part, imag_part)):
                start = local * pieces + part * tiles + tile
                at = local * devices
                send_ref[pl.ds(lead + start, half, stride=size), :] = value[at : at + half]
                keep_ref[pl.ds(start, half, stride=size), :] = value[at + half : at + devices]


def join_kernel(first, unit, used, held_ref, got_ref, send_ref):
    at = 0
    for source in (held_ref, got_ref):
        for start in range(0, first, unit):
            send_ref[at : at + used] = source[start : start + used]
            at += used
    rows = slice(first, first + send_ref.shape[0] - at)
    send_ref[at:] = held_ref[rows] + got_ref[rows]


def fetch_kernel(after_ref, transfer_hbm, transfer_ref, sem):
    copy = pltpu.make_async_copy(transfer_hbm, transfer_ref, sem)
    copy.start()
    copy.wait()


def counts_of(components, comps, base, groups, rows):
    _, lines, parts, _ = tile_of(comps)
    numbers = components.astype(jnp.int32)
    group, place = (numbers - base) >> LANE_BITS, (numbers - base) & (LANES - 1)
    high, low = (numbers >> SPLIT_BITS).astype(jnp.float32), (numbers & (SPLIT - 1)).astype(jnp.float32)
    slot = lax.broadcasted_iota(jnp.int32, (groups, LANES), 0)
    lane = lax.broadcasted_iota(jnp.int32, (LANES, LANES), 0)
    selected, places = [], []
    for tile in range(components.shape[0] // rows):
        for part in range(parts):
            for line in range(lines):
                at = tile * rows + 3 * lines * part + line
                here = group[at : at + 1] == slot
                column = []
                for field in (at + lines, at + 2 * lines):
                    column += [jnp.where(here, value[field : field + 1], 0.0) for value in (high, low)]
                selected.append(jnp.concatenate(column, 0).astype(jnp.bfloat16))
                places.append(jnp.where(place[at : at + 1] == lane, 1.0, 0.0).astype(jnp.bfloat16))
    return lax.dot_general(
        jnp.concatenate(selected, 1), jnp.concatenate(places, 1), NT, preferred_element_type=jnp.float32
    )


def count_kernel(m_local, width, comps, held_ref, count_ref):
    groups = width // LANES
    for local in range(m_local):
        base = (lax.axis_index("ma") * m_local + local) * width
        count_ref[local] = counts_of(held_ref[...], comps, base, groups, tile_of(comps)[3])


def residual_kernel(m_local, pieces, comps, count_ref, held_ref, got_ref, transfer_ref, turned_ref, out_ref):
    width = transfer_ref.shape[3]
    tiles = pieces // 2
    groups = width // LANES
    size = m_local * pieces
    first = got_ref.shape[0] - size
    _, lines, parts, _ = tile_of(comps)
    used = 3 * lines * parts
    spectra = held_ref[...] + got_ref[first:]
    for local in range(m_local):
        base = (lax.axis_index("ma") * m_local + local) * width
        counted = (count_ref[local] + counts_of(got_ref[:first], comps, base, groups, used)).astype(jnp.int32)
        model = []
        for part in range(2):
            high = counted[2 * part * groups : (2 * part + 1) * groups]
            low = counted[(2 * part + 1) * groups : (2 * part + 2) * groups]
            alm = ((high << SPLIT_BITS) + low).astype(jnp.float32) * UNIT
            model.append(jnp.concatenate([alm[g : g + 1] for g in range(groups)], 1))
        model_alm = jnp.concatenate(model, 0).astype(jnp.bfloat16)

        predicted = jnp.concatenate(
            [
                jnp.dot(model_alm, turned_ref[local, :, at : at + BLOCK], preferred_element_type=jnp.float32)
                for at in range(0, 2 * tiles * LANES, BLOCK)
            ],
            1,
        )
        by_real, by_imag = predicted[:, : tiles * LANES], predicted[:, tiles * LANES :]
        pred_real = by_real[0:1] - by_imag[1:2]
        pred_imag = by_real[1:2] + by_imag[0:1]
        start = local * pieces
        spectrum = [
            jnp.concatenate([spectra[start + part * tiles + t : start + part * tiles + t + 1] for t in range(tiles)], 1)
            for part in range(2)
        ]
        resid_real = (spectrum[0] - pred_real).astype(jnp.bfloat16)
        resid_imag = (spectrum[1] - pred_imag).astype(jnp.bfloat16)
        both = jnp.concatenate(
            [jnp.concatenate([resid_real, resid_imag], 1), jnp.concatenate([resid_imag, -resid_real], 1)], 0
        )
        matrix = transfer_ref[local].reshape(2 * tiles * LANES, width)
        for column in range(0, width, BLOCK):
            block = slice(column, column + BLOCK)
            out_ref[local, :, block] = jnp.dot(both, matrix[:, block], preferred_element_type=jnp.float32)


def turn_kernel(after_ref, transfer_ref, turned_ref):
    m_local, _, baselines, _ = transfer_ref.shape
    for local in range(m_local):
        for part in range(2):
            turned_ref[local, :, part * baselines : (part + 1) * baselines] = transfer_ref[local, part].T


def in_hbm(value):
    return pltpu.with_memory_space_constraint(value, pltpu.HBM)


def in_vmem(value):
    return pltpu.with_memory_space_constraint(value, pltpu.VMEM)


def swap(value, offset, devices):
    return lax.ppermute(value, "ma", [(device, device ^ offset) for device in range(devices)])


def body(vis, transfer, band_start, comp_index, comp_amp):
    devices = lax.axis_size("ma")
    samples, _, baselines = vis.shape
    m_local, _, _, width = transfer.shape
    comps = comp_index.shape[0]
    tiles = baselines // LANES
    pieces = 2 * tiles
    size = m_local * pieces
    _, shared_lines, shares, unit = tile_of(comps)
    used = 3 * shared_lines * shares
    vmem, smem, hbm = (pl.BlockSpec(memory_space=space) for space in (pltpu.VMEM, pltpu.SMEM, pltpu.HBM))
    params = pltpu.CompilerParams(vmem_limit_bytes=VMEM_LIMIT)
    lines = vis.reshape(samples, 2, tiles, LANES).transpose(0, 2, 1, 3).reshape(samples * pieces, LANES)
    offsets = offsets_of(devices)
    index, amp = comp_index.reshape(1, comps), comp_amp.T
    index_other = swap(comp_index, offsets[0], devices).reshape(1, comps)
    amp_other = swap(comp_amp, offsets[0], devices).T
    table = pl.pallas_call(
        functools.partial(table_kernel, samples * devices, m_local),
        out_shape=pltpu.VMEM((4 * m_local * devices, samples), jnp.bfloat16),
        in_specs=[smem],
        out_specs=vmem,
        compiler_params=params,
        cost_estimate=pl.CostEstimate(flops=LEAD, transcendentals=0, bytes_accessed=0),
        name="table",
    )(band_start)
    half_rows = devices // 2 * size
    message = pltpu.VMEM((unit + half_rows, LANES), jnp.float32)
    send, kept = pl.pallas_call(
        functools.partial(transform_kernel, samples * devices, m_local),
        out_shape=(message, pltpu.VMEM((half_rows, LANES), jnp.float32)),
        in_specs=[vmem, vmem],
        out_specs=(vmem, vmem),
        compiler_params=params,
        name="transform",
    )(in_vmem(table), in_vmem(lines))
    held = pl.pallas_call(
        pack_kernel,
        out_shape=message,
        in_specs=[vmem, hbm, hbm, vmem, vmem],
        out_specs=vmem,
        scratch_shapes=[
            pltpu.VMEM((1, comps), jnp.int32),
            pltpu.VMEM((2, comps), jnp.int32),
            pltpu.SemaphoreType.DMA((2,)),
        ],
        compiler_params=params,
        name="pack",
    )(in_vmem(kept), in_hbm(index), in_hbm(amp), in_vmem(index_other), in_vmem(amp_other))
    got = swap(send, offsets[0], devices)
    first = unit
    for step, offset in enumerate(offsets[1:], 1):
        going = first + (held.shape[0] - first) // 2
        if step <= 2:
            send = held[:going] + got[:going]
            held = jnp.concatenate([held[:first] + got[:first], held[going:] + got[going:]], 0)
        else:
            parcels = [held[:first], got[:first]]
            if step == len(offsets) - 1:
                count = 2 * first // unit * used + going - first
                send = pl.pallas_call(
                    functools.partial(join_kernel, first, unit, used),
                    out_shape=pltpu.VMEM((count, LANES), jnp.float32),
                    in_specs=[vmem, vmem],
                    out_specs=vmem,
                    compiler_params=params,
                    name="join",
                )(in_vmem(held), in_vmem(got))
            else:
                send = jnp.concatenate(parcels + [held[first:going] + got[first:going]], 0)
            held = jnp.concatenate(parcels + [held[going:] + got[going:]], 0)
            first *= 2
        if step == 1:
            matrices = pl.pallas_call(
                fetch_kernel,
                out_shape=pltpu.VMEM(transfer.shape, transfer.dtype),
                in_specs=[vmem, hbm],
                out_specs=vmem,
                scratch_shapes=[pltpu.SemaphoreType.DMA],
                compiler_params=params,
                name="fetch",
            )(in_vmem(send), in_hbm(transfer))
        got = swap(send, offset, devices)
    components, spectra = held[:first], held[first:]
    count = pl.pallas_call(
        functools.partial(count_kernel, m_local, width, comps),
        out_shape=pltpu.VMEM((m_local, 4 * width // LANES, LANES), jnp.float32),
        in_specs=[vmem],
        out_specs=vmem,
        compiler_params=params,
        name="count",
    )(in_vmem(components))
    turned = pl.pallas_call(
        turn_kernel,
        out_shape=pltpu.VMEM((m_local, width, 2 * baselines), transfer.dtype),
        in_specs=[vmem, vmem],
        out_specs=vmem,
        compiler_params=params,
        name="turn",
    )(in_vmem(components), in_vmem(matrices))
    return pl.pallas_call(
        functools.partial(residual_kernel, m_local, pieces, comps),
        out_shape=jax.ShapeDtypeStruct((m_local, 2, width), jnp.float32),
        in_specs=[vmem] * 5,
        out_specs=vmem,
        compiler_params=params,
        name="residual",
    )(in_vmem(count), in_vmem(spectra), in_vmem(got), in_vmem(matrices), in_vmem(turned))


def solution(mesh):
    in_specs = (
        P(("grp", "ma"), None, None),
        P(("grp", "ma"), None, None, None),
        P("grp"),
        P(("grp", "ma")),
        P(("grp", "ma"), None),
    )
    out_specs = P(("grp", "ma"), None, None)
    return jax.shard_map(body, mesh=mesh, in_specs=in_specs, out_specs=out_specs, check_vma=False)
```
